32 devices in a mesh: les: 8 (over y, x, core), modes: 4 (over z).
Axes of the slice: x: 2, y: 2, z: 4, core: 2. Of those that a mesh axis runs over, the one named last changes fastest.
Arguments:
- pressure: bfloat16 [65536, 512], P('les', 'modes'), may hold values from -6 to 6
- targets: int32 [65536], P('les'), may hold values from 0 to 32767, as said below
- counts: int32 [8], P('les'), may hold values from 1 to 8192, as said below
- pseudo_inverse: bfloat16 [2, 1536, 16384], P(None, None, ('les', 'modes')), may hold values from -0.046875 to 0.046875
Outputs:
- harmonics: float32 [2, 2, 8, 1536], P(None, None, None, ('les', 'modes'))
The draws below stay inside these ranges and needn't reach their ends.
Inputs may be any that keep to these rules, and one draw needn't show every extreme that they name: `counts`: some partition holds exactly 8192 live faces; all partitions together hold 32768. `targets`: the live slots (slot f of partition i with f < counts[i]) name every station point exactly once. Point p of a station lies in the point rows of les index p // (512 * 4); at most 1024 live faces of one partition lie in the point rows of one les index, and some partition reaches that bound. Slots that are not live hold arbitrary indices in the range.
All inputs are finite; a program needn't handle non-finite values.
Results may differ from the reference program's by a relative error of at most 0.0003.
Values may be sent and summed in bfloat16 or wider, within the bound.
A program may use at most 64 MiB of HBM per device.

```python
import math
import jax
import jax.numpy as jnp
from jax import lax

STATIONS = 2
MODES = 1536
TIME = 512
HARM = 8
PT_DEV = 512
POINTS = 16384
FACE_CAP = 8192
N_LES = 8
N_MODES = 4


def face_layout(key):
    rows_les = PT_DEV * N_MODES
    per_owner = STATIONS * rows_les
    key_busy, key_spread, key_shuffle, key_dead, key_order = jax.random.split(jax.random.fold_in(key, 11), 5)
    busiest = jax.random.randint(key_busy, (), 0, N_LES)
    spread = jax.random.randint(key_spread, (per_owner,), 0, N_LES - 1)
    spread = spread + (spread >= busiest).astype(jnp.int32)
    partition_ids = jnp.arange(N_LES, dtype=jnp.int32)
    removed = jnp.sum((spread[:, None] == partition_ids[None, :]).astype(jnp.int32), axis=0)
    counts = per_owner - removed + per_owner * (partition_ids == busiest).astype(jnp.int32)
    offsets = jnp.cumsum(counts) - counts
    slot_ids = jnp.arange(FACE_CAP, dtype=jnp.int32)
    face_ranks = offsets[:, None] + slot_ids[None, :]
    is_alive = slot_ids[None, :] < counts[:, None]
    owner_les = face_ranks % N_LES
    within = jnp.minimum(face_ranks // N_LES, per_owner - 1)
    shuffles = jax.vmap(lambda sub_key: jax.random.permutation(sub_key, per_owner))(jax.random.split(key_shuffle, N_LES))
    chosen = shuffles[owner_les, within]
    station_ids = chosen // rows_les
    point_ids = owner_les * rows_les + chosen % rows_les
    live_targets = (station_ids * POINTS + point_ids).astype(jnp.int32)
    slot_order = jax.vmap(lambda sub_key: jax.random.permutation(sub_key, FACE_CAP))(jax.random.split(key_order, N_LES))
    scores = jnp.where(is_alive, slot_order, slot_order + FACE_CAP).astype(jnp.int32)
    order = jnp.argsort(scores, axis=1, stable=True).astype(jnp.int32)
    shuffled = jnp.take_along_axis(live_targets, order, axis=1)
    dead_targets = jax.random.randint(key_dead, (N_LES, FACE_CAP), 0, STATIONS * POINTS)
    targets = jnp.where(is_alive, shuffled, dead_targets).reshape(N_LES * FACE_CAP)
    return (counts.astype(jnp.int32), targets.astype(jnp.int32))


def draw_counts(key, part):
    return face_layout(key)[0]


def draw_targets(key, part):
    return face_layout(key)[1]


def block_scale(key, extent, cuts, smallest, high):
    level = 1.0
    for axis_at, parts in cuts:
        steps = jax.random.uniform(jax.random.fold_in(jax.random.fold_in(key, 6), axis_at), (parts,), jnp.float32, smallest / len(cuts), high / len(cuts))
        level = level * jnp.repeat(jnp.exp(steps), extent[axis_at] // parts).reshape((-1,) + (1,) * (len(extent) - 1 - axis_at))
    return level


def bell_draw(stream_key, dims, width, limit, pieces=(), held_as=jnp.bfloat16):
    entries = jax.random.normal(stream_key, dims, jnp.float32) * width
    if len(pieces) > 0:
        entries = block_scale(stream_key, dims, pieces, -0.22, 0.18) * entries
    return jnp.clip(entries, min=-limit, max=limit).astype(held_as)


def setup_inputs(seed: int = 0) -> dict:
    streams_of = jax.random.split(jax.random.key(seed), 5)
    return {
        "pressure": bell_draw(streams_of[0], (N_LES * FACE_CAP, TIME), 1.0, 6.0, ((0, 8), (1, 4))),
        "targets": draw_targets(jax.random.fold_in(streams_of[4], 71), 0),
        "counts": draw_counts(jax.random.fold_in(streams_of[4], 71), 0),
        "pseudo_inverse": bell_draw(streams_of[3], (STATIONS, MODES, POINTS), POINTS ** -0.5, 0.046875, ((2, 32),)),
    }


def fourier_rows():
    sample_ids = jnp.arange(TIME, dtype=jnp.int32)
    orders = jnp.arange(1, HARM + 1, dtype=jnp.int32)
    phase_ids = orders[:, None] * sample_ids[None, :] % TIME
    angles = phase_ids.astype(jnp.float32) * (2.0 * math.pi / TIME)
    scale_factor = math.sqrt(2.0 / TIME)
    return jnp.stack([jnp.cos(angles), -jnp.sin(angles)]) * scale_factor

def reference(pressure, targets, counts, pseudo_inverse):
    slot_ids = jnp.arange(N_LES * FACE_CAP, dtype=jnp.int32)
    partition = slot_ids // FACE_CAP
    is_live = slot_ids % FACE_CAP < counts[partition]
    rows = jnp.where(is_live, targets, STATIONS * POINTS).astype(jnp.int32)
    station = jnp.zeros((STATIONS * POINTS, TIME), jnp.bfloat16).at[rows].set(pressure, mode='drop')
    fourier = fourier_rows()
    spectra = jnp.einsum('ckt,pt->ckp', fourier, station.astype(jnp.float32), precision=lax.Precision.HIGHEST)
    row_span = POINTS // N_LES
    results = []
    for station_index in range(STATIONS):

        def add_block(block_index, totals, station_index=station_index):
            start = (station_index * POINTS + block_index * row_span).astype(jnp.int32)
            spectra_part = lax.dynamic_slice_in_dim(spectra, start, row_span, 2)
            offset = (block_index * row_span).astype(jnp.int32)
            weights = lax.dynamic_slice_in_dim(pseudo_inverse[station_index], offset, row_span, 1).astype(jnp.float32)
            return totals + jnp.einsum('ckp,mp->ckm', spectra_part, weights, precision=lax.Precision.HIGHEST)
        results.append(lax.fori_loop(0, N_LES, add_block, jnp.zeros((2, HARM, MODES), jnp.float32)))
    return jnp.stack(results)
```

```python
import functools
import math

import jax
import jax.numpy as jnp
import numpy as np
from jax import lax
from jax.experimental import pallas as pl
from jax.experimental.pallas import tpu as pltpu
from jax.sharding import PartitionSpec as P

TIME = 512
HARM = 8
COLS = 2 * HARM
LANES = 128
GROUPS = LANES // COLS
GROUP_LINES = 8
VMEM_BYTES = 56 * 1024 * 1024
MESH = pl.DeviceIdType.MESH
F32 = jnp.float32
BF16 = jnp.bfloat16


def fourier_columns():
    phase_ids = np.arange(TIME)[:, None] * np.arange(1, HARM + 1)[None, :] % TIME
    angles = phase_ids * (2.0 * math.pi / TIME)
    columns = np.concatenate([np.cos(angles), -np.sin(angles)], axis=1) * math.sqrt(2.0 / TIME)
    columns = np.tile(columns, (1, GROUPS)).astype(np.float32)
    high = columns.astype(jnp.bfloat16)
    low = (columns - high.astype(np.float32)).astype(jnp.bfloat16)
    return np.stack([high, low])


def partner(index, step, count):
    total, bit = 0, 1
    while bit < count:
        total = total + lax.rem(lax.rem(lax.div(index, bit), 2) + (step // bit) % 2, 2) * bit
        bit *= 2
    return total


def pick(rows):
    group = lax.broadcasted_iota(jnp.int32, (1, LANES), 1) // COLS
    bit = 1
    while len(rows) > 1:
        even = (group // bit) % 2 == 0
        rows = [jnp.where(even, rows[at], rows[at + 1]) for at in range(0, len(rows), 2)]
        bit *= 2
    return rows[0]


def split(value):
    high = value.astype(BF16)
    return high, (value - high.astype(F32)).astype(BF16)


def share_start(les, les_width, tiles, span):
    return jnp.minimum(lax.div(les * les_width, LANES), tiles - span)


def kernel(
    les_count, mode_count, counts_hbm, targets_hbm, pressure_hbm, basis_hbm, pinv_hbm, out,
    counts, targets, pressure, basis, weights, lines_of, lanes_of, rows_of, points_of, ranks_of,
    groups_of, sources, table, table_in, table_own, inverse, source_ids, point_ids,
    spectra, packed, data_in, spread, blocks, blocks_in, product, sums_in, shares, last_in,
    load_sem, smem_sem, table_send, table_recv, data_send, data_recv,
    block_send, block_recv, sum_send, sum_recv, last_send, last_recv,
):
    les, mode = lax.axis_index("les"), lax.axis_index("modes")
    face_slots, block_len = pressure.shape
    stations, mode_total, point_dev = weights.shape
    rows_les = point_dev * mode_count
    points_all = rows_les * les_count
    lines = face_slots // LANES
    cap = face_slots // les_count
    tag_rows = cap // LANES
    rank_rows = cap // GROUPS
    dense = stations * rows_les // LANES
    mode_lines = point_dev // LANES
    block_rows = point_dev // GROUPS
    les_steps = range(les_count - 1, 0, -1)
    mode_steps = range(mode_count - 1, 0, -1)

    times = pl.ds(pl.multiple_of(mode * block_len, block_len), block_len)
    loads = [
        pltpu.make_async_copy(targets_hbm, targets, load_sem.at[0]),
        pltpu.make_async_copy(counts_hbm, counts, load_sem.at[1]),
        pltpu.make_async_copy(pressure_hbm, pressure, load_sem.at[2]),
        pltpu.make_async_copy(basis_hbm.at[0, times], basis.at[pl.ds(0, block_len)], load_sem.at[3]),
        pltpu.make_async_copy(
            basis_hbm.at[1, times], basis.at[pl.ds(block_len, block_len)], load_sem.at[4]
        ),
        pltpu.make_async_copy(pinv_hbm, weights, load_sem.at[5]),
    ]
    for load in loads:
        load.start()
    barrier = pltpu.get_barrier_semaphore()
    for step in les_steps:
        peer = partner(les, step, les_count)
        pl.semaphore_signal(barrier, inc=1, device_id=(peer, mode), device_id_type=MESH)
    for step in mode_steps:
        peer = partner(mode, step, mode_count)
        pl.semaphore_signal(barrier, inc=1, device_id=(les, peer), device_id_type=MESH)
    loads[0].wait()
    loads[1].wait()

    target = targets[...]
    point = lax.rem(target, points_all)
    station = lax.div(target, points_all)
    owner = lax.div(point, rows_les)
    name = station * rows_les + lax.rem(point, rows_les)
    line = lax.broadcasted_iota(jnp.int32, (lines, LANES), 0)
    lane = lax.broadcasted_iota(jnp.int32, (lines, LANES), 1)
    live = line * LANES + lane < counts[0]
    owner = jnp.where(live, owner, les_count)
    first = lax.broadcasted_iota(jnp.int32, (LANES, 2 * LANES), 0)
    second = lax.broadcasted_iota(jnp.int32, (LANES, 2 * LANES), 1)
    upper = jnp.where((first <= second) | (second >= LANES), 1.0, 0.0).astype(BF16)
    above = lax.broadcasted_iota(jnp.int32, (lines, lines), 0)
    below = lax.broadcasted_iota(jnp.int32, (lines, lines), 1)
    earlier = jnp.where(above > below, 1.0, 0.0).astype(BF16)
    matches = [owner == at for at in range(les_count)]
    stacked = jnp.concatenate([jnp.where(m, 1.0, 0.0).astype(BF16) for m in matches], axis=0)
    running = jnp.dot(stacked, upper, preferred_element_type=F32)
    totals = [running[at * lines:(at + 1) * lines, LANES:] for at in range(les_count)]
    before = jnp.dot(
        earlier, jnp.concatenate(totals, axis=1).astype(BF16), preferred_element_type=F32
    )
    rank = jnp.zeros((lines, LANES), F32)
    for at in range(les_count):
        here = running[at * lines:(at + 1) * lines, :LANES] + before[:, at * LANES:(at + 1) * LANES]
        rank = jnp.where(matches[at], here, rank)
    rank = rank.astype(jnp.int32) - 1
    lines_of[...] = jnp.where(live, owner * tag_rows + lax.div(rank, LANES), -1)
    lanes_of[...] = lax.rem(rank, LANES)
    rows_of[...] = jnp.where(live, owner * dense + lax.div(name, LANES), -1)
    points_of[...] = lax.rem(name, LANES)
    ranks_of[...] = (lax.div(rank, GROUPS) + 1).astype(F32)
    groups_of[...] = lax.rem(rank, GROUPS).astype(F32)

    send_lines = les_count * tag_rows
    send_ids = lax.broadcasted_iota(jnp.int32, (send_lines, LANES), 0)
    lane_ids = lax.broadcasted_iota(jnp.int32, (LANES, LANES), 0)
    face_lane = lax.broadcasted_iota(jnp.int32, (LANES, LANES), 1).astype(F32)
    over_lanes = (((1,), (1,)), ((), ()))

    def add_sources(step, total):
        lefts, rights = [], []
        for at in range(GROUP_LINES):
            line_at = step * GROUP_LINES + at
            hit = lane_ids == lanes_of[pl.ds(line_at, 1), :]
            left = send_ids == lines_of[pl.ds(line_at, 1), :]
            face_line = jnp.full((1, LANES), line_at, jnp.int32).astype(F32)
            lefts.append(jnp.where(left, 1.0, 0.0).astype(BF16))
            rights.append(jnp.concatenate(
                [jnp.where(hit, face_line, 0.0), jnp.where(hit, face_lane, 0.0)], axis=0
            ).astype(BF16))
        return total + lax.dot_general(
            jnp.concatenate(lefts, axis=1), jnp.concatenate(rights, axis=1), over_lanes,
            preferred_element_type=F32,
        )

    total = lax.fori_loop(
        0, lines // GROUP_LINES, add_sources, jnp.zeros((send_lines, 2 * LANES), F32)
    )
    source = (total[:, :LANES] * LANES + total[:, LANES:]).astype(jnp.int32)
    sources[...] = jnp.clip(source, 0, face_slots - 1)
    source_copy = pltpu.make_async_copy(sources, source_ids, smem_sem.at[0])
    source_copy.start()

    table_lines = les_count * dense
    table_ids = lax.broadcasted_iota(jnp.int32, (table_lines, LANES), 0)
    table[...] = jnp.zeros((table_lines, 2 * LANES), F32)

    @pl.loop(0, lines // GROUP_LINES)
    def _(step):
        lefts, rights = [], []
        for at in range(GROUP_LINES):
            line_at = step * GROUP_LINES + at
            hit = lane_ids == points_of[pl.ds(line_at, 1), :]
            left = table_ids == rows_of[pl.ds(line_at, 1), :]
            lefts.append(jnp.where(left, 1.0, 0.0).astype(BF16))
            rights.append(jnp.concatenate(
                [
                    jnp.where(hit, ranks_of[pl.ds(line_at, 1), :], 0.0),
                    jnp.where(hit, groups_of[pl.ds(line_at, 1), :], 0.0),
                ], axis=0
            ).astype(BF16))
        table[...] += lax.dot_general(
            jnp.concatenate(lefts, axis=1), jnp.concatenate(rights, axis=1), over_lanes,
            preferred_element_type=F32,
        )

    table_own[...] = table[:, :LANES] + table[:, LANES:] * rank_rows
    pl.semaphore_wait(barrier, les_count + mode_count - 2)

    def owned(peer):
        return pl.ds(pl.multiple_of(peer * dense, dense), dense)

    def table_copy(step):
        peer = partner(les, step, les_count)
        return pltpu.make_async_remote_copy(
            src_ref=table_own.at[owned(peer)],
            dst_ref=table_in.at[step],
            send_sem=table_send.at[step],
            recv_sem=table_recv.at[step],
            device_id=(peer, mode),
            device_id_type=MESH,
        )

    for step in les_steps:
        table_copy(step).start()

    chunk = math.gcd(face_slots, 1024)
    for load in loads[2:5]:
        load.wait()
    block_basis = basis[...]

    @pl.loop(0, face_slots // chunk)
    def _(step):
        at = pl.ds(pl.multiple_of(step * chunk, chunk), chunk)
        block = pressure[at, :]
        block = jnp.concatenate([block, block], axis=1)
        spectra[at, :] = jnp.dot(block, block_basis, preferred_element_type=F32)

    source_copy.wait()

    def data_copy(step):
        peer = partner(les, step, les_count)
        return pltpu.make_async_remote_copy(
            src_ref=packed.at[step],
            dst_ref=data_in.at[step],
            send_sem=data_send.at[step],
            recv_sem=data_recv.at[step],
            device_id=(peer, mode),
            device_id_type=MESH,
        )

    def fill(step, place):
        peer = partner(les, step, les_count)

        @pl.loop(0, tag_rows)
        def _(part):
            from_line = peer * tag_rows + part
            for row in range(COLS):
                ids = [source_ids[from_line, row * GROUPS + at] for at in range(GROUPS)]
                values = [spectra[pl.ds(face, 1), :] for face in ids]
                place[step, pl.ds(part * COLS + row, 1), :] = pick(values)

    @pl.loop(0, les_count - 1)
    def _(back):
        step = les_count - 1 - back
        fill(step, packed)
        data_copy(step).start()

    fill(0, data_in)

    found = jnp.zeros((dense, LANES), F32)
    for step in range(les_count):
        if step == 0:
            part = table_own[owned(les), :]
        else:
            table_copy(step).wait()
            part = table_in[step]
        found = jnp.where(part > 0.0, part + float(step * cap - 1), found)
    inverse[...] = jnp.clip(found.astype(jnp.int32), 0, face_slots - 1)
    inverse_copy = pltpu.make_async_copy(inverse, point_ids, smem_sem.at[1])
    inverse_copy.start()

    from_lane = lax.broadcasted_iota(jnp.int32, (LANES, GROUPS * LANES), 0)
    to_lane = lax.broadcasted_iota(jnp.int32, (LANES, GROUPS * LANES), 1)
    wanted = (to_lane // LANES) * COLS + to_lane % COLS
    repeat = jnp.where(from_lane == wanted, 1.0, 0.0).astype(BF16)
    repeat = jnp.concatenate([repeat, repeat], axis=0)
    for step in (*les_steps, 0):
        if step > 0:
            data_copy(step).wait()
        high, low = split(data_in[step])
        wide = jnp.dot(jnp.concatenate([high, low], axis=1), repeat, preferred_element_type=F32)
        for at in range(GROUPS):
            spread[pl.ds(step * cap + at * rank_rows, rank_rows), :] = (
                wide[:, at * LANES:(at + 1) * LANES]
            )
    inverse_copy.wait()

    def block_copy(of, step):
        return pltpu.make_async_remote_copy(
            src_ref=blocks.at[of, step],
            dst_ref=blocks_in.at[of, step],
            send_sem=block_send.at[of, step],
            recv_sem=block_recv.at[of, step],
            device_id=(les, partner(mode, step, mode_count)),
            device_id_type=MESH,
        )

    def gather(of, step):
        peer = partner(mode, step, mode_count)
        start = (of * mode_count + peer) * mode_lines
        halves = LANES // block_rows

        @pl.loop(0, block_rows // 8)
        def _(part):
            for row in range(8):
                ids = [
                    point_ids[start + at // halves, at % halves * block_rows + part * 8 + row]
                    for at in range(GROUPS)
                ]
                values = [spread[pl.ds(place, 1), :] for place in ids]
                blocks[of, step, pl.ds(part * 8 + row, 1), :] = pick(values)

    for of in range(stations):
        for step in mode_steps:
            gather(of, step)
            block_copy(of, step).start()
        gather(of, 0)

    loads[5].wait()
    tiles = mode_total // LANES
    width = out.shape[2]
    les_width = mode_count * width
    span = sums_in.shape[2]

    def sum_copy(of, step):
        peer = partner(les, step, les_count)
        start = share_start(peer, les_width, tiles, span)
        return pltpu.make_async_remote_copy(
            src_ref=product.at[of, pl.ds(start, span)],
            dst_ref=sums_in.at[of, step],
            send_sem=sum_send.at[of, step],
            recv_sem=sum_recv.at[of, step],
            device_id=(peer, mode),
            device_id_type=MESH,
        )

    for of in range(stations):
        total = blocks[of, 0]
        for step in mode_steps:
            block_copy(of, step).wait()
            total = total + blocks_in[of, step]
        high = total.astype(BF16).astype(F32)
        turned = []
        for half in (high, total - high):
            both = jnp.concatenate([half, pltpu.roll(half, LANES - COLS, 1)], axis=0).T
            pairs = [both[at * COLS:(at + 1) * COLS, :] for at in range(0, GROUPS, 2)]
            turned.append(jnp.concatenate(pairs, axis=1))
        turned = jnp.concatenate(turned, axis=0).astype(BF16)
        result = lax.dot_general(turned, weights[of], over_lanes, preferred_element_type=F32)
        result = result[:COLS] + result[COLS:]
        for tile in range(tiles):
            product[of, tile] = result[:, tile * LANES:(tile + 1) * LANES]
        for step in les_steps:
            sum_copy(of, step).start()

    own_start = share_start(les, les_width, tiles, span)
    own = []
    for of in range(stations):
        total = product[of, pl.ds(own_start, span)]
        for step in les_steps:
            sum_copy(of, step).wait()
            total = total + sums_in[of, step]
        own.append(jnp.concatenate([total[at] for at in range(span)], axis=1))

    offset = les * les_width - own_start * LANES
    lane = lax.broadcasted_iota(jnp.int32, (COLS, LANES), 1)

    def last_copy(step):
        return pltpu.make_async_remote_copy(
            src_ref=shares.at[step],
            dst_ref=last_in.at[step],
            send_sem=last_send.at[step],
            recv_sem=last_recv.at[step],
            device_id=(les, partner(mode, step, mode_count)),
            device_id_type=MESH,
        )

    for step in (*mode_steps, 0):
        at = offset + partner(mode, step, mode_count) * width
        turn = lax.rem(span * LANES - at, span * LANES)
        one = pltpu.roll(own[0], turn, 1)[:, :LANES]
        two = pltpu.roll(own[1], lax.rem(turn + width, span * LANES), 1)[:, :LANES]
        shares[step] = jnp.where(lane < width, one, two)
        if step > 0:
            last_copy(step).start()
    total = shares[0]
    for step in mode_steps:
        last_copy(step).wait()
        total = total + last_in[step]
    out[0] = total[:, :width]
    out[1] = pltpu.roll(total, LANES - width, 1)[:, :width]


def local(pressure, targets, counts, pseudo_inverse):
    les_count = lax.axis_size("les")
    mode_count = lax.axis_size("modes")
    face_slots, block_len = pressure.shape
    stations, mode_total, point_dev = pseudo_inverse.shape
    lines = face_slots // LANES
    cap = face_slots // les_count
    rank_rows = cap // GROUPS
    send_lines = les_count * cap // LANES
    dense = stations * point_dev * mode_count // LANES
    block_rows = point_dev // GROUPS
    width = mode_total // (les_count * mode_count)
    les_width = width * mode_count
    tiles = mode_total // LANES
    span = max(
        ((at + 1) * les_width - 1) // LANES - at * les_width // LANES + 1 for at in range(les_count)
    )
    anywhere = pl.BlockSpec(memory_space=pl.ANY)
    dma = pltpu.SemaphoreType.DMA
    vmem = pltpu.VMEM
    result = pl.pallas_call(
        functools.partial(kernel, les_count, mode_count),
        out_shape=jax.ShapeDtypeStruct((stations, COLS, width), F32),
        in_specs=[anywhere] * 5,
        out_specs=pl.BlockSpec(memory_space=pltpu.VMEM),
        scratch_shapes=[
            pltpu.SMEM((1,), jnp.int32),
            vmem((lines, LANES), jnp.int32),
            vmem((face_slots, block_len), BF16),
            vmem((2 * block_len, LANES), BF16),
            vmem((stations, mode_total, point_dev), BF16),
            vmem((lines, LANES), jnp.int32),
            vmem((lines, LANES), jnp.int32),
            vmem((lines, LANES), jnp.int32),
            vmem((lines, LANES), jnp.int32),
            vmem((lines, LANES), F32),
            vmem((lines, LANES), F32),
            vmem((send_lines, LANES), jnp.int32),
            vmem((les_count * dense, 2 * LANES), F32),
            vmem((les_count, dense, LANES), F32),
            vmem((les_count * dense, LANES), F32),
            vmem((dense, LANES), jnp.int32),
            pltpu.SMEM((send_lines, LANES), jnp.int32),
            pltpu.SMEM((dense, LANES), jnp.int32),
            vmem((face_slots, LANES), F32),
            vmem((les_count, rank_rows, LANES), F32),
            vmem((les_count, rank_rows, LANES), F32),
            vmem((les_count * cap, LANES), F32),
            vmem((stations, mode_count, block_rows, LANES), F32),
            vmem((stations, mode_count, block_rows, LANES), F32),
            vmem((stations, tiles, COLS, LANES), F32),
            vmem((stations, les_count, span, COLS, LANES), F32),
            vmem((mode_count, COLS, LANES), F32),
            vmem((mode_count, COLS, LANES), F32),
            dma((6,)),
            dma((2,)),
            dma((les_count,)),
            dma((les_count,)),
            dma((les_count,)),
            dma((les_count,)),
            dma((stations, mode_count)),
            dma((stations, mode_count)),
            dma((stations, les_count)),
            dma((stations, les_count)),
            dma((mode_count,)),
            dma((mode_count,)),
        ],
        compiler_params=pltpu.CompilerParams(
            collective_id=0, has_side_effects=True, vmem_limit_bytes=VMEM_BYTES
        ),
        name="harmonics",
    )(
        counts, targets.reshape(lines, LANES), pressure,
        jnp.asarray(fourier_columns()), pseudo_inverse,
    )
    return result.reshape(stations, 2, HARM, width)


def solution(mesh):
    placed = (P("les", "modes"), P("les"), P("les"), P(None, None, ("les", "modes")))
    return jax.shard_map(
        local,
        mesh=mesh,
        in_specs=placed,
        out_specs=P(None, None, None, ("les", "modes")),
        check_vma=False,
    )
```

```python
import functools
import math

import jax
import jax.numpy as jnp
import numpy as np
from jax import lax
from jax.experimental import pallas as pl
from jax.experimental.pallas import tpu as pltpu
from jax.sharding import PartitionSpec as P

TIME = 512
HARM = 8
COLS = 2 * HARM
LANES = 128
GROUPS = LANES // COLS
GROUP_LINES = 8
VMEM_BYTES = 56 * 1024 * 1024
MESH = pl.DeviceIdType.MESH
F32 = jnp.float32
BF16 = jnp.bfloat16


def fourier_columns():
    phase_ids = np.arange(TIME)[:, None] * np.arange(1, HARM + 1)[None, :] % TIME
    angles = phase_ids * (2.0 * math.pi / TIME)
    columns = np.concatenate([np.cos(angles), -np.sin(angles)], axis=1) * math.sqrt(2.0 / TIME)
    columns = np.tile(columns, (1, GROUPS)).astype(np.float32)
    high = columns.astype(jnp.bfloat16)
    low = (columns - high.astype(np.float32)).astype(jnp.bfloat16)
    return np.stack([high, low])


def partner(index, step, count):
    total, bit = 0, 1
    while bit < count:
        total = total + lax.rem(lax.rem(lax.div(index, bit), 2) + (step // bit) % 2, 2) * bit
        bit *= 2
    return total


def pick(rows):
    group = lax.broadcasted_iota(jnp.int32, (1, LANES), 1) // COLS
    bit = 1
    while len(rows) > 1:
        even = (group // bit) % 2 == 0
        rows = [jnp.where(even, rows[at], rows[at + 1]) for at in range(0, len(rows), 2)]
        bit *= 2
    return rows[0]


def split(value):
    high = value.astype(BF16)
    return high, (value - high.astype(F32)).astype(BF16)


def group_rows(rows):
    return rows * GROUPS // LANES


def coded(rows):
    return rows // 2 + group_rows(rows)


def encode(value):
    rows = value.shape[0]
    top = jnp.abs(value)
    for shift in (1, 2, 4, 8):
        top = jnp.maximum(top, pltpu.roll(top, LANES - shift, 1))
    from_lane = lax.broadcasted_iota(jnp.int32, (LANES, LANES), 0)
    to_lane = lax.broadcasted_iota(jnp.int32, (LANES, LANES), 1)
    widen = jnp.where(from_lane == to_lane // COLS * COLS, 1.0, 0.0).astype(BF16)
    top = jnp.dot((top * 1.01).astype(BF16), widen, preferred_element_type=F32)
    exponent = jnp.ceil(jnp.log2(jnp.maximum(top, 1e-30)))
    scale = jnp.exp2(-exponent).astype(BF16).astype(F32) * 32767.0
    code = (value * scale + 32768.5).astype(jnp.int32)
    code = jnp.clip(code, 0, 65535)
    words = (code[:rows // 2] << 16) | code[rows // 2:]
    group = lax.broadcasted_iota(jnp.int32, (GROUPS, LANES), 0)
    lane = lax.broadcasted_iota(jnp.int32, (GROUPS, LANES), 1)
    choose = jnp.where(lane == group * COLS, 1.0, 0.0).astype(BF16)
    narrow = lax.dot_general(
        choose, exponent.astype(BF16), (((1,), (1,)), ((), ())), preferred_element_type=F32
    ).astype(jnp.int32)
    lines = group_rows(rows)
    narrow = [narrow[at:at + lines] for at in range(0, GROUPS, lines)]
    return words, narrow[0] if len(narrow) == 1 else jnp.concatenate(narrow, axis=1)


def decode(words, exponents):
    rows = 2 * words.shape[0]
    narrow = [exponents[:, at:at + rows] for at in range(0, LANES, rows)]
    narrow = narrow[0] if len(narrow) == 1 else jnp.concatenate(narrow, axis=0)
    scale = jnp.exp2(narrow.astype(F32)).astype(BF16)
    group = lax.broadcasted_iota(jnp.int32, (GROUPS, LANES), 0)
    lane = lax.broadcasted_iota(jnp.int32, (GROUPS, LANES), 1)
    widen = jnp.where(lane // COLS == group, 1.0, 0.0).astype(BF16)
    scale = lax.dot_general(
        scale, widen, (((0,), (0,)), ((), ())), preferred_element_type=F32
    ) * (1.0 / 32767.0)
    high, low = lax.shift_right_logical(words, 16), words & 65535
    return (jnp.concatenate([high, low], axis=0) - 32768).astype(F32) * scale


def add_places(line_count, lines_of, lanes_of, extras, out_lines):
    out_ids = lax.broadcasted_iota(jnp.int32, (out_lines, LANES), 0)
    lane_ids = lax.broadcasted_iota(jnp.int32, (LANES, LANES), 0)
    entry_lane = lax.broadcasted_iota(jnp.int32, (LANES, LANES), 1).astype(F32)
    parts = 2 + len(extras)

    def add(step, total):
        lefts, rights = [], []
        for at in range(GROUP_LINES):
            line_at = step * GROUP_LINES + at
            hit = lane_ids == lanes_of[pl.ds(line_at, 1), :]
            left = out_ids == lines_of[pl.ds(line_at, 1), :]
            entry_line = jnp.full((1, LANES), line_at, jnp.int32).astype(F32)
            values = [entry_line, entry_lane] + [ref[pl.ds(line_at, 1), :] for ref in extras]
            lefts.append(jnp.where(left, 1.0, 0.0).astype(BF16))
            rights.append(
                jnp.concatenate([jnp.where(hit, value, 0.0) for value in values], axis=0).astype(BF16)
            )
        return total + lax.dot_general(
            jnp.concatenate(lefts, axis=1), jnp.concatenate(rights, axis=1),
            (((1,), (1,)), ((), ())), preferred_element_type=F32,
        )

    total = lax.fori_loop(
        0, line_count // GROUP_LINES, add, jnp.zeros((out_lines, parts * LANES), F32)
    )
    return [total[:, at * LANES:(at + 1) * LANES] for at in range(parts)]


def share_start(les, les_width, tiles, span):
    return jnp.minimum(lax.div(les * les_width, LANES), tiles - span)


def kernel(
    les_count, mode_count, counts_hbm, targets_hbm, pressure_hbm, basis_hbm, pinv_hbm, out,
    counts, targets, pressure, basis, weights, lines_of, lanes_of, names_high, names_low,
    sources, tags, tags_in, tag_lines, tag_lanes, inverse, source_ids, point_ids,
    spectra, placed, packed, data_in, spread, blocks, packed_blocks, blocks_in,
    product, sums_in, shares, last_in,
    load_sem, smem_sem, tag_send, tag_recv, data_send, data_recv,
    block_send, block_recv, sum_send, sum_recv, last_send, last_recv,
):
    les, mode = lax.axis_index("les"), lax.axis_index("modes")
    face_slots, block_len = pressure.shape
    stations, mode_total, point_dev = weights.shape
    rows_les = point_dev * mode_count
    points_all = rows_les * les_count
    lines = face_slots // LANES
    cap = face_slots // les_count
    tag_rows = cap // LANES
    rank_rows = cap // GROUPS
    dense = stations * rows_les // LANES
    mode_lines = point_dev // LANES
    block_rows = point_dev // GROUPS
    les_steps = range(les_count - 1, 0, -1)
    mode_steps = range(mode_count - 1, 0, -1)

    times = pl.ds(pl.multiple_of(mode * block_len, block_len), block_len)
    loads = [
        pltpu.make_async_copy(targets_hbm, targets, load_sem.at[0]),
        pltpu.make_async_copy(counts_hbm, counts, load_sem.at[1]),
        pltpu.make_async_copy(pressure_hbm, pressure, load_sem.at[2]),
        pltpu.make_async_copy(basis_hbm.at[0, times], basis.at[pl.ds(0, block_len)], load_sem.at[3]),
        pltpu.make_async_copy(
            basis_hbm.at[1, times], basis.at[pl.ds(block_len, block_len)], load_sem.at[4]
        ),
        pltpu.make_async_copy(pinv_hbm, weights, load_sem.at[5]),
    ]
    for load in loads:
        load.start()
    barrier = pltpu.get_barrier_semaphore()
    for step in les_steps:
        peer = partner(les, step, les_count)
        pl.semaphore_signal(barrier, inc=1, device_id=(peer, mode), device_id_type=MESH)
    for step in mode_steps:
        peer = partner(mode, step, mode_count)
        pl.semaphore_signal(barrier, inc=1, device_id=(les, peer), device_id_type=MESH)
    loads[0].wait()
    loads[1].wait()

    target = targets[...]
    point = lax.rem(target, points_all)
    station = lax.div(target, points_all)
    owner = lax.div(point, rows_les)
    name = station * rows_les + lax.rem(point, rows_les)
    line = lax.broadcasted_iota(jnp.int32, (lines, LANES), 0)
    lane = lax.broadcasted_iota(jnp.int32, (lines, LANES), 1)
    live = line * LANES + lane < counts[0]
    owner = jnp.where(live, owner, les_count)
    first = lax.broadcasted_iota(jnp.int32, (LANES, 2 * LANES), 0)
    second = lax.broadcasted_iota(jnp.int32, (LANES, 2 * LANES), 1)
    upper = jnp.where((first <= second) | (second >= LANES), 1.0, 0.0).astype(BF16)
    above = lax.broadcasted_iota(jnp.int32, (lines, lines), 0)
    below = lax.broadcasted_iota(jnp.int32, (lines, lines), 1)
    earlier = jnp.where(above > below, 1.0, 0.0).astype(BF16)
    matches = [owner == at for at in range(les_count)]
    stacked = jnp.concatenate([jnp.where(m, 1.0, 0.0).astype(BF16) for m in matches], axis=0)
    running = jnp.dot(stacked, upper, preferred_element_type=F32)
    totals = [running[at * lines:(at + 1) * lines, LANES:] for at in range(les_count)]
    before = jnp.dot(
        earlier, jnp.concatenate(totals, axis=1).astype(BF16), preferred_element_type=F32
    )
    rank = jnp.zeros((lines, LANES), F32)
    for at in range(les_count):
        here = running[at * lines:(at + 1) * lines, :LANES] + before[:, at * LANES:(at + 1) * LANES]
        rank = jnp.where(matches[at], here, rank)
    rank = rank.astype(jnp.int32) - 1
    lines_of[...] = jnp.where(live, owner * tag_rows + lax.div(rank, LANES), -1)
    lanes_of[...] = lax.rem(rank, LANES)
    names_high[...] = lax.div(name + 1, 64).astype(F32)
    names_low[...] = lax.rem(name + 1, 64).astype(F32)

    from_line, from_lane, high, low = add_places(
        lines, lines_of, lanes_of, (names_high, names_low), les_count * tag_rows
    )
    source = jnp.clip((from_line * LANES + from_lane).astype(jnp.int32), 0, face_slots - 1)
    tag = (high * 64 + low).astype(jnp.int32)
    for at in range(les_count):
        sources[at] = source[at * tag_rows:(at + 1) * tag_rows]
        tags[at] = tag[at * tag_rows:(at + 1) * tag_rows]

    def id_copy(step, slot):
        return pltpu.make_async_copy(
            sources.at[partner(les, step, les_count)], source_ids.at[slot], smem_sem.at[slot]
        )

    id_copy(les_count - 1, 0).start()
    id_copy(les_count - 2, 1).start()

    chunk = math.gcd(face_slots, 1024)
    for load in loads[2:5]:
        load.wait()
    block_basis = basis[...]

    @pl.loop(0, face_slots // chunk)
    def _(step):
        at = pl.ds(pl.multiple_of(step * chunk, chunk), chunk)
        block = pressure[at, :]
        block = jnp.concatenate([block, block], axis=1)
        spectra[at, :] = jnp.dot(block, block_basis, preferred_element_type=F32)

    pl.semaphore_wait(barrier, les_count + mode_count - 2)

    def tag_copy(step):
        peer = partner(les, step, les_count)
        return pltpu.make_async_remote_copy(
            src_ref=tags.at[peer],
            dst_ref=tags_in.at[step],
            send_sem=tag_send.at[step],
            recv_sem=tag_recv.at[step],
            device_id=(peer, mode),
            device_id_type=MESH,
        )

    def data_copy(step):
        peer = partner(les, step, les_count)
        return pltpu.make_async_remote_copy(
            src_ref=packed.at[step],
            dst_ref=data_in.at[step],
            send_sem=data_send.at[step],
            recv_sem=data_recv.at[step],
            device_id=(peer, mode),
            device_id_type=MESH,
        )

    for step in les_steps:
        tag_copy(step).start()

    def fill(step, slot):
        for row in range(rank_rows):
            ranks = [at * rank_rows + row for at in range(GROUPS)]
            ids = [source_ids[slot, at // LANES, at % LANES] for at in ranks]
            placed[slot, pl.ds(row, 1), :] = pick([spectra[pl.ds(face, 1), :] for face in ids])
        words, exponents = encode(placed[slot])
        packed[step, pl.ds(0, rank_rows // 2), :] = words
        packed[step, pl.ds(rank_rows // 2, group_rows(rank_rows)), :] = exponents

    @pl.loop(0, les_count // 2)
    def _(pair):
        for slot in range(2):
            step = les_count - 1 - slot - 2 * pair
            id_copy(step, slot).wait()
            fill(step, slot)

            @pl.when(pair < les_count // 2 - 1)
            def _(step=step, slot=slot):
                id_copy(step - 2, slot).start()

            if slot == 0:
                data_copy(step).start()
            else:

                @pl.when(step > 0)
                def _(step=step):
                    data_copy(step).start()

    for step in range(les_count):
        if step > 0:
            tag_copy(step).wait()
        found = (tags[les] if step == 0 else tags_in[step]) - 1
        at = pl.ds(step * tag_rows, tag_rows)
        tag_lines[at, :] = found >> 7
        tag_lanes[at, :] = found & (LANES - 1)
    from_line, from_lane = add_places(les_count * tag_rows, tag_lines, tag_lanes, (), dense)
    found = (from_line * LANES + from_lane).astype(jnp.int32)
    inverse[...] = jnp.clip(found, 0, les_count * cap - 1)
    inverse_copy = pltpu.make_async_copy(inverse, point_ids, smem_sem.at[2])
    inverse_copy.start()

    from_lane = lax.broadcasted_iota(jnp.int32, (LANES, GROUPS * LANES), 0)
    to_lane = lax.broadcasted_iota(jnp.int32, (LANES, GROUPS * LANES), 1)
    wanted = (to_lane // LANES) * COLS + to_lane % COLS
    repeat = jnp.where(from_lane == wanted, 1.0, 0.0).astype(BF16)
    repeat = jnp.concatenate([repeat, repeat], axis=0)
    for step in (*les_steps, 0):
        if step > 0:
            data_copy(step).wait()
        held = data_in if step > 0 else packed
        received = decode(
            held[step, pl.ds(0, rank_rows // 2), :],
            held[step, pl.ds(rank_rows // 2, group_rows(rank_rows)), :],
        )
        high, low = split(received)
        wide = jnp.dot(jnp.concatenate([high, low], axis=1), repeat, preferred_element_type=F32)
        for at in range(GROUPS):
            spread[pl.ds(step * cap + at * rank_rows, rank_rows), :] = (
                wide[:, at * LANES:(at + 1) * LANES]
            )
    inverse_copy.wait()

    def block_copy(of, step):
        return pltpu.make_async_remote_copy(
            src_ref=packed_blocks.at[of, step],
            dst_ref=blocks_in.at[of, step],
            send_sem=block_send.at[of, step],
            recv_sem=block_recv.at[of, step],
            device_id=(les, partner(mode, step, mode_count)),
            device_id_type=MESH,
        )

    def gather(of, step):
        peer = partner(mode, step, mode_count)
        start = (of * mode_count + peer) * mode_lines
        halves = LANES // block_rows

        @pl.loop(0, block_rows // 8)
        def _(part):
            for row in range(8):
                ids = [
                    point_ids[start + at // halves, at % halves * block_rows + part * 8 + row]
                    for at in range(GROUPS)
                ]
                values = [spread[pl.ds(place, 1), :] for place in ids]
                blocks[of, step, pl.ds(part * 8 + row, 1), :] = pick(values)

    for of in range(stations):
        for step in mode_steps:
            gather(of, step)
            words, exponents = encode(blocks[of, step])
            packed_blocks[of, step, pl.ds(0, block_rows // 2), :] = words
            packed_blocks[of, step, pl.ds(block_rows // 2, group_rows(block_rows)), :] = exponents
            block_copy(of, step).start()
        gather(of, 0)

    loads[5].wait()
    tiles = mode_total // LANES
    width = out.shape[2]
    les_width = mode_count * width
    span = sums_in.shape[2]

    def sum_copy(of, step):
        peer = partner(les, step, les_count)
        start = share_start(peer, les_width, tiles, span)
        return pltpu.make_async_remote_copy(
            src_ref=product.at[of, pl.ds(start, span)],
            dst_ref=sums_in.at[of, step],
            send_sem=sum_send.at[of, step],
            recv_sem=sum_recv.at[of, step],
            device_id=(peer, mode),
            device_id_type=MESH,
        )

    for of in range(stations):
        total = blocks[of, 0]
        for step in mode_steps:
            block_copy(of, step).wait()
            total = total + decode(
                blocks_in[of, step, pl.ds(0, block_rows // 2), :],
                blocks_in[of, step, pl.ds(block_rows // 2, group_rows(block_rows)), :],
            )
        high = total.astype(BF16).astype(F32)
        turned = []
        for half in (high, total - high):
            both = jnp.concatenate([half, pltpu.roll(half, LANES - COLS, 1)], axis=0).T
            pairs = [both[at * COLS:(at + 1) * COLS, :] for at in range(0, GROUPS, 2)]
            turned.append(jnp.concatenate(pairs, axis=1))
        turned = jnp.concatenate(turned, axis=0).astype(BF16)
        result = lax.dot_general(
            turned, weights[of], (((1,), (1,)), ((), ())), preferred_element_type=F32
        )
        result = result[:COLS] + result[COLS:]
        for tile in range(tiles):
            product[of, tile] = result[:, tile * LANES:(tile + 1) * LANES]
        for step in les_steps:
            sum_copy(of, step).start()

    own_start = share_start(les, les_width, tiles, span)
    own = []
    for of in range(stations):
        total = product[of, pl.ds(own_start, span)]
        for step in les_steps:
            sum_copy(of, step).wait()
            total = total + sums_in[of, step]
        own.append(jnp.concatenate([total[at] for at in range(span)], axis=1))

    offset = les * les_width - own_start * LANES
    lane = lax.broadcasted_iota(jnp.int32, (COLS, LANES), 1)

    def last_copy(step):
        return pltpu.make_async_remote_copy(
            src_ref=shares.at[step],
            dst_ref=last_in.at[step],
            send_sem=last_send.at[step],
            recv_sem=last_recv.at[step],
            device_id=(les, partner(mode, step, mode_count)),
            device_id_type=MESH,
        )

    for step in (*mode_steps, 0):
        at = offset + partner(mode, step, mode_count) * width
        turn = lax.rem(span * LANES - at, span * LANES)
        one = pltpu.roll(own[0], turn, 1)[:, :LANES]
        two = pltpu.roll(own[1], lax.rem(turn + width, span * LANES), 1)[:, :LANES]
        shares[step] = jnp.where(lane < width, one, two)
        if step > 0:
            last_copy(step).start()
    total = shares[0]
    for step in mode_steps:
        last_copy(step).wait()
        total = total + last_in[step]
    out[0] = total[:, :width]
    out[1] = pltpu.roll(total, LANES - width, 1)[:, :width]


def local(pressure, targets, counts, pseudo_inverse):
    les_count = lax.axis_size("les")
    mode_count = lax.axis_size("modes")
    face_slots, block_len = pressure.shape
    stations, mode_total, point_dev = pseudo_inverse.shape
    lines = face_slots // LANES
    cap = face_slots // les_count
    rank_rows = cap // GROUPS
    tag_rows = cap // LANES
    dense = stations * point_dev * mode_count // LANES
    block_rows = point_dev // GROUPS
    width = mode_total // (les_count * mode_count)
    les_width = width * mode_count
    tiles = mode_total // LANES
    span = max(
        ((at + 1) * les_width - 1) // LANES - at * les_width // LANES + 1 for at in range(les_count)
    )
    anywhere = pl.BlockSpec(memory_space=pl.ANY)
    dma = pltpu.SemaphoreType.DMA
    vmem = pltpu.VMEM
    result = pl.pallas_call(
        functools.partial(kernel, les_count, mode_count),
        out_shape=jax.ShapeDtypeStruct((stations, COLS, width), F32),
        in_specs=[anywhere] * 5,
        out_specs=pl.BlockSpec(memory_space=pltpu.VMEM),
        scratch_shapes=[
            pltpu.SMEM((1,), jnp.int32),
            vmem((lines, LANES), jnp.int32),
            vmem((face_slots, block_len), BF16),
            vmem((2 * block_len, LANES), BF16),
            vmem((stations, mode_total, point_dev), BF16),
            vmem((lines, LANES), jnp.int32),
            vmem((lines, LANES), jnp.int32),
            vmem((lines, LANES), F32),
            vmem((lines, LANES), F32),
            vmem((les_count, tag_rows, LANES), jnp.int32),
            vmem((les_count, tag_rows, LANES), jnp.int32),
            vmem((les_count, tag_rows, LANES), jnp.int32),
            vmem((les_count * tag_rows, LANES), jnp.int32),
            vmem((les_count * tag_rows, LANES), jnp.int32),
            vmem((dense, LANES), jnp.int32),
            pltpu.SMEM((2, tag_rows, LANES), jnp.int32),
            pltpu.SMEM((dense, LANES), jnp.int32),
            vmem((face_slots, LANES), F32),
            vmem((2, rank_rows, LANES), F32),
            vmem((les_count, coded(rank_rows), LANES), jnp.int32),
            vmem((les_count, coded(rank_rows), LANES), jnp.int32),
            vmem((les_count * cap, LANES), F32),
            vmem((stations, mode_count, block_rows, LANES), F32),
            vmem((stations, mode_count, coded(block_rows), LANES), jnp.int32),
            vmem((stations, mode_count, coded(block_rows), LANES), jnp.int32),
            vmem((stations, tiles, COLS, LANES), F32),
            vmem((stations, les_count, span, COLS, LANES), F32),
            vmem((mode_count, COLS, LANES), F32),
            vmem((mode_count, COLS, LANES), F32),
            dma((6,)),
            dma((3,)),
            dma((les_count,)),
            dma((les_count,)),
            dma((les_count,)),
            dma((les_count,)),
            dma((stations, mode_count)),
            dma((stations, mode_count)),
            dma((stations, les_count)),
            dma((stations, les_count)),
            dma((mode_count,)),
            dma((mode_count,)),
        ],
        compiler_params=pltpu.CompilerParams(
            collective_id=0, has_side_effects=True, vmem_limit_bytes=VMEM_BYTES
        ),
        name="harmonics",
    )(
        counts, targets.reshape(lines, LANES), pressure,
        jnp.asarray(fourier_columns()), pseudo_inverse,
    )
    return result.reshape(stations, 2, HARM, width)


def solution(mesh):
    placed = (P("les", "modes"), P("les"), P("les"), P(None, None, ("les", "modes")))
    return jax.shard_map(
        local,
        mesh=mesh,
        in_specs=placed,
        out_specs=P(None, None, None, ("les", "modes")),
        check_vma=False,
    )
```

```python
import functools
import math

import jax
import jax.numpy as jnp
import numpy as np
from jax import lax
from jax.experimental import pallas as pl
from jax.experimental.pallas import tpu as pltpu
from jax.sharding import PartitionSpec as P

TIME = 512
HARM = 8
COLS = 2 * HARM
LANES = 128
GROUPS = LANES // COLS
GROUP_LINES = 8
VMEM_BYTES = 56 * 1024 * 1024
MESH = pl.DeviceIdType.MESH
F32 = jnp.float32
BF16 = jnp.bfloat16


def fourier_columns():
    phase_ids = np.arange(TIME)[:, None] * np.arange(1, HARM + 1)[None, :] % TIME
    angles = phase_ids * (2.0 * math.pi / TIME)
    columns = np.concatenate([np.cos(angles), -np.sin(angles)], axis=1) * math.sqrt(2.0 / TIME)
    columns = np.tile(columns, (1, GROUPS)).astype(np.float32)
    high = columns.astype(jnp.bfloat16)
    low = (columns - high.astype(np.float32)).astype(jnp.bfloat16)
    return np.stack([high, low])


def partner(index, step, count):
    total, bit = 0, 1
    while bit < count:
        total = total + lax.rem(lax.rem(lax.div(index, bit), 2) + (step // bit) % 2, 2) * bit
        bit *= 2
    return total


def pick(rows):
    group = lax.broadcasted_iota(jnp.int32, (1, LANES), 1) // COLS
    bit = 1
    while len(rows) > 1:
        even = (group // bit) % 2 == 0
        rows = [jnp.where(even, rows[at], rows[at + 1]) for at in range(0, len(rows), 2)]
        bit *= 2
    return rows[0]


def split(value):
    high = value.astype(BF16)
    return high, (value - high.astype(F32)).astype(BF16)


def add_places(line_count, lines_of, lanes_of, extras, out_lines):
    out_ids = lax.broadcasted_iota(jnp.int32, (out_lines, LANES), 0)
    lane_ids = lax.broadcasted_iota(jnp.int32, (LANES, LANES), 0)
    entry_lane = lax.broadcasted_iota(jnp.int32, (LANES, LANES), 1).astype(F32)
    parts = 2 + len(extras)

    def add(step, total):
        lefts, rights = [], []
        for at in range(GROUP_LINES):
            line_at = step * GROUP_LINES + at
            hit = lane_ids == lanes_of[pl.ds(line_at, 1), :]
            left = out_ids == lines_of[pl.ds(line_at, 1), :]
            entry_line = jnp.full((1, LANES), line_at, jnp.int32).astype(F32)
            values = [entry_line, entry_lane] + [ref[pl.ds(line_at, 1), :] for ref in extras]
            lefts.append(jnp.where(left, 1.0, 0.0).astype(BF16))
            rights.append(
                jnp.concatenate([jnp.where(hit, value, 0.0) for value in values], axis=0).astype(BF16)
            )
        return total + lax.dot_general(
            jnp.concatenate(lefts, axis=1), jnp.concatenate(rights, axis=1),
            (((1,), (1,)), ((), ())), preferred_element_type=F32,
        )

    total = lax.fori_loop(
        0, line_count // GROUP_LINES, add, jnp.zeros((out_lines, parts * LANES), F32)
    )
    return [total[:, at * LANES:(at + 1) * LANES] for at in range(parts)]


def share_start(les, les_width, tiles, span):
    return jnp.minimum(lax.div(les * les_width, LANES), tiles - span)


def kernel(
    les_count, mode_count, counts_hbm, targets_hbm, pressure_hbm, basis_hbm, pinv_hbm, out,
    counts, targets, pressure, basis, weights, lines_of, lanes_of, names_high, names_low,
    sources, tags, tags_in, tag_lines, tag_lanes, inverse, ordered, source_ids, point_ids,
    spectra, packed, data_in, spread, blocks, blocks_in,
    product, sums_in, shares, last_in,
    load_sem, smem_sem, tag_send, tag_recv, data_send, data_recv,
    block_send, block_recv, sum_send, sum_recv, last_send, last_recv,
):
    les, mode = lax.axis_index("les"), lax.axis_index("modes")
    face_slots, block_len = pressure.shape
    stations, mode_total, point_dev = weights.shape
    rows_les = point_dev * mode_count
    points_all = rows_les * les_count
    lines = face_slots // LANES
    cap = face_slots // les_count
    tag_rows = cap // LANES
    rank_rows = cap // GROUPS
    dense = stations * rows_les // LANES
    mode_lines = point_dev // LANES
    block_rows = point_dev // GROUPS
    les_steps = range(les_count - 1, 0, -1)
    mode_steps = range(mode_count - 1, 0, -1)

    times = pl.ds(pl.multiple_of(mode * block_len, block_len), block_len)
    loads = [
        pltpu.make_async_copy(targets_hbm, targets, load_sem.at[0]),
        pltpu.make_async_copy(counts_hbm, counts, load_sem.at[1]),
        pltpu.make_async_copy(pressure_hbm, pressure, load_sem.at[2]),
        pltpu.make_async_copy(basis_hbm.at[0, times], basis.at[pl.ds(0, block_len)], load_sem.at[3]),
        pltpu.make_async_copy(
            basis_hbm.at[1, times], basis.at[pl.ds(block_len, block_len)], load_sem.at[4]
        ),
        pltpu.make_async_copy(pinv_hbm, weights, load_sem.at[5]),
    ]
    for load in loads:
        load.start()
    barrier = pltpu.get_barrier_semaphore()
    for step in les_steps:
        peer = partner(les, step, les_count)
        pl.semaphore_signal(barrier, inc=1, device_id=(peer, mode), device_id_type=MESH)
    for step in mode_steps:
        peer = partner(mode, step, mode_count)
        pl.semaphore_signal(barrier, inc=1, device_id=(les, peer), device_id_type=MESH)
    loads[0].wait()
    loads[1].wait()

    target = targets[...]
    point = lax.rem(target, points_all)
    station = lax.div(target, points_all)
    owner = lax.div(point, rows_les)
    name = station * rows_les + lax.rem(point, rows_les)
    line = lax.broadcasted_iota(jnp.int32, (lines, LANES), 0)
    lane = lax.broadcasted_iota(jnp.int32, (lines, LANES), 1)
    live = line * LANES + lane < counts[0]
    owner = jnp.where(live, owner, les_count)
    first = lax.broadcasted_iota(jnp.int32, (LANES, 2 * LANES), 0)
    second = lax.broadcasted_iota(jnp.int32, (LANES, 2 * LANES), 1)
    upper = jnp.where((first <= second) | (second >= LANES), 1.0, 0.0).astype(BF16)
    above = lax.broadcasted_iota(jnp.int32, (lines, lines), 0)
    below = lax.broadcasted_iota(jnp.int32, (lines, lines), 1)
    earlier = jnp.where(above > below, 1.0, 0.0).astype(BF16)
    matches = [owner == at for at in range(les_count)]
    stacked = jnp.concatenate([jnp.where(m, 1.0, 0.0).astype(BF16) for m in matches], axis=0)
    running = jnp.dot(stacked, upper, preferred_element_type=F32)
    totals = [running[at * lines:(at + 1) * lines, LANES:] for at in range(les_count)]
    before = jnp.dot(
        earlier, jnp.concatenate(totals, axis=1).astype(BF16), preferred_element_type=F32
    )
    rank = jnp.zeros((lines, LANES), F32)
    for at in range(les_count):
        here = running[at * lines:(at + 1) * lines, :LANES] + before[:, at * LANES:(at + 1) * LANES]
        rank = jnp.where(matches[at], here, rank)
    rank = rank.astype(jnp.int32) - 1
    lines_of[...] = jnp.where(live, owner * tag_rows + lax.div(rank, LANES), -1)
    lanes_of[...] = lax.rem(rank, LANES)
    names_high[...] = lax.div(name + 1, 64).astype(F32)
    names_low[...] = lax.rem(name + 1, 64).astype(F32)

    from_line, from_lane, high, low = add_places(
        lines, lines_of, lanes_of, (names_high, names_low), les_count * tag_rows
    )
    source = jnp.clip((from_line * LANES + from_lane).astype(jnp.int32), 0, face_slots - 1)
    tag = (high * 64 + low).astype(jnp.int32)
    for at in range(les_count):
        sources[at] = source[at * tag_rows:(at + 1) * tag_rows]
        tags[at] = tag[at * tag_rows:(at + 1) * tag_rows]

    def id_copy(step, slot):
        return pltpu.make_async_copy(
            sources.at[partner(les, step, les_count)], source_ids.at[slot], smem_sem.at[slot]
        )

    id_copy(les_count - 1, 0).start()
    id_copy(les_count - 2, 1).start()

    chunk = math.gcd(face_slots, 1024)
    for load in loads[2:5]:
        load.wait()
    block_basis = basis[...]

    @pl.loop(0, face_slots // chunk)
    def _(step):
        at = pl.ds(pl.multiple_of(step * chunk, chunk), chunk)
        block = pressure[at, :]
        block = jnp.concatenate([block, block], axis=1)
        spectra[at, :] = jnp.dot(block, block_basis, preferred_element_type=F32)

    pl.semaphore_wait(barrier, les_count + mode_count - 2)

    def tag_copy(step):
        peer = partner(les, step, les_count)
        return pltpu.make_async_remote_copy(
            src_ref=tags.at[peer],
            dst_ref=tags_in.at[step],
            send_sem=tag_send.at[step],
            recv_sem=tag_recv.at[step],
            device_id=(peer, mode),
            device_id_type=MESH,
        )

    def data_copy(step):
        peer = partner(les, step, les_count)
        return pltpu.make_async_remote_copy(
            src_ref=packed.at[step],
            dst_ref=data_in.at[step],
            send_sem=data_send.at[step],
            recv_sem=data_recv.at[step],
            device_id=(peer, mode),
            device_id_type=MESH,
        )

    for step in les_steps:
        tag_copy(step).start()

    def fill(step, slot):
        for row in range(rank_rows):
            ranks = [at * rank_rows + row for at in range(GROUPS)]
            ids = [source_ids[slot, at // LANES, at % LANES] for at in ranks]
            packed[step, pl.ds(row, 1), :] = pick([spectra[pl.ds(face, 1), :] for face in ids])

    @pl.loop(0, les_count // 2)
    def _(pair):
        for slot in range(2):
            step = les_count - 1 - slot - 2 * pair
            id_copy(step, slot).wait()
            fill(step, slot)

            @pl.when(pair < les_count // 2 - 1)
            def _(step=step, slot=slot):
                id_copy(step - 2, slot).start()

            if slot == 0:
                data_copy(step).start()
            else:

                @pl.when(step > 0)
                def _(step=step):
                    data_copy(step).start()

    for step in range(les_count):
        if step > 0:
            tag_copy(step).wait()
        found = (tags[les] if step == 0 else tags_in[step]) - 1
        at = pl.ds(step * tag_rows, tag_rows)
        tag_lines[at, :] = found >> 7
        tag_lanes[at, :] = found & (LANES - 1)
    from_line, from_lane = add_places(les_count * tag_rows, tag_lines, tag_lanes, (), dense)
    found = (from_line * LANES + from_lane).astype(jnp.int32)
    inverse[...] = jnp.clip(found, 0, les_count * cap - 1)
    for of in range(stations):
        for step in range(mode_count):
            start = (of * mode_count + partner(mode, step, mode_count)) * mode_lines
            ordered[pl.ds((of * mode_count + step) * mode_lines, mode_lines), :] = (
                inverse[pl.ds(start, mode_lines), :]
            )
    inverse_copy = pltpu.make_async_copy(ordered, point_ids, smem_sem.at[2])
    inverse_copy.start()

    from_lane = lax.broadcasted_iota(jnp.int32, (LANES, GROUPS * LANES), 0)
    to_lane = lax.broadcasted_iota(jnp.int32, (LANES, GROUPS * LANES), 1)
    wanted = (to_lane // LANES) * COLS + to_lane % COLS
    repeat = jnp.where(from_lane == wanted, 1.0, 0.0).astype(BF16)
    repeat = jnp.concatenate([repeat, repeat], axis=0)
    for step in (*les_steps, 0):
        if step > 0:
            data_copy(step).wait()
        high, low = split(data_in[step] if step > 0 else packed[0])
        wide = jnp.dot(jnp.concatenate([high, low], axis=1), repeat, preferred_element_type=F32)
        for at in range(GROUPS):
            spread[pl.ds(step * cap + at * rank_rows, rank_rows), :] = (
                wide[:, at * LANES:(at + 1) * LANES]
            )
    inverse_copy.wait()

    def block_copy(of, step):
        return pltpu.make_async_remote_copy(
            src_ref=blocks.at[of, step],
            dst_ref=blocks_in.at[of, step],
            send_sem=block_send.at[of, step],
            recv_sem=block_recv.at[of, step],
            device_id=(les, partner(mode, step, mode_count)),
            device_id_type=MESH,
        )

    def gather(of, step):
        start = (of * mode_count + step) * mode_lines
        for row in range(block_rows):
            points = [at * block_rows + row for at in range(GROUPS)]
            ids = [point_ids[start + at // LANES, at % LANES] for at in points]
            blocks[of, step, pl.ds(row, 1), :] = pick([spread[pl.ds(place, 1), :] for place in ids])

    for of in range(stations):
        for step in mode_steps:
            gather(of, step)
            block_copy(of, step).start()
        gather(of, 0)

    loads[5].wait()
    tiles = mode_total // LANES
    width = out.shape[2]
    les_width = mode_count * width
    span = sums_in.shape[2]

    def sum_copy(of, step):
        peer = partner(les, step, les_count)
        start = share_start(peer, les_width, tiles, span)
        return pltpu.make_async_remote_copy(
            src_ref=product.at[of, pl.ds(start, span)],
            dst_ref=sums_in.at[of, step],
            send_sem=sum_send.at[of, step],
            recv_sem=sum_recv.at[of, step],
            device_id=(peer, mode),
            device_id_type=MESH,
        )

    for of in range(stations):
        total = blocks[of, 0]
        for step in mode_steps:
            block_copy(of, step).wait()
            total = total + blocks_in[of, step]
        high = total.astype(BF16).astype(F32)
        turned = []
        for half in (high, total - high):
            both = jnp.concatenate([half, pltpu.roll(half, LANES - COLS, 1)], axis=0).T
            pairs = [both[at * COLS:(at + 1) * COLS, :] for at in range(0, GROUPS, 2)]
            turned.append(jnp.concatenate(pairs, axis=1))
        turned = jnp.concatenate(turned, axis=0).astype(BF16)
        result = lax.dot_general(
            turned, weights[of], (((1,), (1,)), ((), ())), preferred_element_type=F32
        )
        result = result[:COLS] + result[COLS:]
        for tile in range(tiles):
            product[of, tile] = result[:, tile * LANES:(tile + 1) * LANES]
        for step in les_steps:
            sum_copy(of, step).start()

    own_start = share_start(les, les_width, tiles, span)
    own = []
    for of in range(stations):
        total = product[of, pl.ds(own_start, span)]
        for step in les_steps:
            sum_copy(of, step).wait()
            total = total + sums_in[of, step]
        own.append(jnp.concatenate([total[at] for at in range(span)], axis=1))

    offset = les * les_width - own_start * LANES
    lane = lax.broadcasted_iota(jnp.int32, (COLS, LANES), 1)

    def last_copy(step):
        return pltpu.make_async_remote_copy(
            src_ref=shares.at[step],
            dst_ref=last_in.at[step],
            send_sem=last_send.at[step],
            recv_sem=last_recv.at[step],
            device_id=(les, partner(mode, step, mode_count)),
            device_id_type=MESH,
        )

    for step in (*mode_steps, 0):
        at = offset + partner(mode, step, mode_count) * width
        turn = lax.rem(span * LANES - at, span * LANES)
        one = pltpu.roll(own[0], turn, 1)[:, :LANES]
        two = pltpu.roll(own[1], lax.rem(turn + width, span * LANES), 1)[:, :LANES]
        shares[step] = jnp.where(lane < width, one, two)
        if step > 0:
            last_copy(step).start()
    total = shares[0]
    for step in mode_steps:
        last_copy(step).wait()
        total = total + last_in[step]
    out[0] = total[:, :width]
    out[1] = pltpu.roll(total, LANES - width, 1)[:, :width]


def local(pressure, targets, counts, pseudo_inverse):
    les_count = lax.axis_size("les")
    mode_count = lax.axis_size("modes")
    face_slots, block_len = pressure.shape
    stations, mode_total, point_dev = pseudo_inverse.shape
    lines = face_slots // LANES
    cap = face_slots // les_count
    rank_rows = cap // GROUPS
    tag_rows = cap // LANES
    dense = stations * point_dev * mode_count // LANES
    block_rows = point_dev // GROUPS
    width = mode_total // (les_count * mode_count)
    les_width = width * mode_count
    tiles = mode_total // LANES
    span = max(
        ((at + 1) * les_width - 1) // LANES - at * les_width // LANES + 1 for at in range(les_count)
    )
    anywhere = pl.BlockSpec(memory_space=pl.ANY)
    dma = pltpu.SemaphoreType.DMA
    vmem = pltpu.VMEM
    result = pl.pallas_call(
        functools.partial(kernel, les_count, mode_count),
        out_shape=jax.ShapeDtypeStruct((stations, COLS, width), F32),
        in_specs=[anywhere] * 5,
        out_specs=pl.BlockSpec(memory_space=pltpu.VMEM),
        scratch_shapes=[
            pltpu.SMEM((1,), jnp.int32),
            vmem((lines, LANES), jnp.int32),
            vmem((face_slots, block_len), BF16),
            vmem((2 * block_len, LANES), BF16),
            vmem((stations, mode_total, point_dev), BF16),
            vmem((lines, LANES), jnp.int32),
            vmem((lines, LANES), jnp.int32),
            vmem((lines, LANES), F32),
            vmem((lines, LANES), F32),
            vmem((les_count, tag_rows, LANES), jnp.int32),
            vmem((les_count, tag_rows, LANES), jnp.int32),
            vmem((les_count, tag_rows, LANES), jnp.int32),
            vmem((les_count * tag_rows, LANES), jnp.int32),
            vmem((les_count * tag_rows, LANES), jnp.int32),
            vmem((dense, LANES), jnp.int32),
            vmem((dense, LANES), jnp.int32),
            pltpu.SMEM((2, tag_rows, LANES), jnp.int32),
            pltpu.SMEM((dense, LANES), jnp.int32),
            vmem((face_slots, LANES), F32),
            vmem((les_count, rank_rows, LANES), F32),
            vmem((les_count, rank_rows, LANES), F32),
            vmem((les_count * cap, LANES), F32),
            vmem((stations, mode_count, block_rows, LANES), F32),
            vmem((stations, mode_count, block_rows, LANES), F32),
            vmem((stations, tiles, COLS, LANES), F32),
            vmem((stations, les_count, span, COLS, LANES), F32),
            vmem((mode_count, COLS, LANES), F32),
            vmem((mode_count, COLS, LANES), F32),
            dma((6,)),
            dma((3,)),
            dma((les_count,)),
            dma((les_count,)),
            dma((les_count,)),
            dma((les_count,)),
            dma((stations, mode_count)),
            dma((stations, mode_count)),
            dma((stations, les_count)),
            dma((stations, les_count)),
            dma((mode_count,)),
            dma((mode_count,)),
        ],
        compiler_params=pltpu.CompilerParams(
            collective_id=0, has_side_effects=True, vmem_limit_bytes=VMEM_BYTES
        ),
        name="harmonics",
    )(
        counts, targets.reshape(lines, LANES), pressure,
        jnp.asarray(fourier_columns()), pseudo_inverse,
    )
    return result.reshape(stations, 2, HARM, width)


def solution(mesh):
    placed = (P("les", "modes"), P("les"), P("les"), P(None, None, ("les", "modes")))
    return jax.shard_map(
        local,
        mesh=mesh,
        in_specs=placed,
        out_specs=P(None, None, None, ("les", "modes")),
        check_vma=False,
    )
```

```python
import functools
import math

import jax
import jax.numpy as jnp
import numpy as np
from jax import lax
from jax.experimental import pallas as pl
from jax.experimental.pallas import tpu as pltpu
from jax.sharding import PartitionSpec as P

TIME = 512
HARM = 8
COLS = 2 * HARM
LANES = 128
GROUPS = LANES // COLS
GROUP_LINES = 64
WIDEN = 4
VMEM_BYTES = 56 * 1024 * 1024
MESH = pl.DeviceIdType.MESH
F32 = jnp.float32
BF16 = jnp.bfloat16


def fourier_columns():
    phase_ids = np.arange(TIME)[:, None] * np.arange(1, HARM + 1)[None, :] % TIME
    angles = phase_ids * (2.0 * math.pi / TIME)
    columns = np.concatenate([np.cos(angles), -np.sin(angles)], axis=1) * math.sqrt(2.0 / TIME)
    columns = np.tile(columns, (1, GROUPS)).astype(np.float32)
    high = columns.astype(jnp.bfloat16)
    low = (columns - high.astype(np.float32)).astype(jnp.bfloat16)
    return np.stack([high, low])


def partner(index, step, count):
    total, bit = 0, 1
    while bit < count:
        total = total + lax.rem(lax.rem(lax.div(index, bit), 2) + (step // bit) % 2, 2) * bit
        bit *= 2
    return total


def pick(rows):
    group = lax.broadcasted_iota(jnp.int32, (1, LANES), 1) // COLS
    bit = 1
    while len(rows) > 1:
        even = (group // bit) % 2 == 0
        rows = [jnp.where(even, rows[at], rows[at + 1]) for at in range(0, len(rows), 2)]
        bit *= 2
    return rows[0]


def split(value):
    high = value.astype(BF16)
    return high, (value - high.astype(F32)).astype(BF16)


def add_places(line_count, lines_of, lanes_of, values_of, out_lines):
    out_ids = lax.broadcasted_iota(jnp.int32, (out_lines, LANES), 0).astype(F32).astype(BF16)
    lane_ids = lax.broadcasted_iota(jnp.int32, (LANES, LANES), 0).astype(F32).astype(BF16)
    one, zero = jnp.ones((), BF16), jnp.zeros((), BF16)

    def add(step, total):
        lefts, rights = [], []
        for at in range(GROUP_LINES):
            line_at = step * GROUP_LINES + at

            def spread_row(row, rows):
                return jnp.broadcast_to(row.astype(BF16), (rows, LANES))

            hit = lane_ids == spread_row(lanes_of[pl.ds(line_at, 1), :], LANES)
            left = out_ids == spread_row(lines_of[pl.ds(line_at, 1), :], out_lines)
            values = [spread_row(row, out_lines) for row in values_of(line_at)]
            lefts.append(jnp.concatenate([jnp.where(left, value, zero) for value in values], axis=0))
            rights.append(jnp.where(hit, one, zero))
        return total + lax.dot_general(
            jnp.concatenate(rights, axis=1), jnp.concatenate(lefts, axis=1),
            (((1,), (1,)), ((), ())), preferred_element_type=F32,
        )

    total = lax.fori_loop(
        0, line_count // GROUP_LINES, add, jnp.zeros((LANES, 2 * out_lines), F32)
    ).T
    return (total[:out_lines] * LANES + total[out_lines:]).astype(jnp.int32)


def slot_values(line_at):
    line = jnp.full((1, LANES), line_at, jnp.int32).astype(F32)
    return line, lax.broadcasted_iota(jnp.int32, (1, LANES), 1).astype(F32)


def share_start(les, les_width, tiles, span):
    return jnp.minimum(lax.div(les * les_width, LANES), tiles - span)


def kernel(
    les_count, mode_count, counts_hbm, targets_hbm, pressure_hbm, basis_hbm, pinv_hbm, out,
    counts, targets, pressure, basis, weights, lines_of, lanes_of, names_high, names_low,
    sources, tags, tags_in, tag_lines, tag_lanes, inverse, ordered, source_ids, point_ids,
    spectra, packed, data_in, spread, blocks, blocks_in,
    product, sums_in, shares, last_in,
    load_sem, smem_sem, tag_send, tag_recv, data_send, data_recv,
    block_send, block_recv, sum_send, sum_recv, last_send, last_recv,
):
    les, mode = lax.axis_index("les"), lax.axis_index("modes")
    face_slots, block_len = pressure.shape
    stations, mode_total, point_dev = weights.shape
    rows_les = point_dev * mode_count
    points_all = rows_les * les_count
    lines = face_slots // LANES
    cap = face_slots // les_count
    tag_rows = cap // LANES
    rank_rows = cap // GROUPS
    dense = stations * rows_les // LANES
    mode_lines = point_dev // LANES
    block_rows = point_dev // GROUPS
    les_steps = range(les_count - 1, 0, -1)
    mode_steps = range(mode_count - 1, 0, -1)

    times = pl.ds(pl.multiple_of(mode * block_len, block_len), block_len)
    loads = [
        pltpu.make_async_copy(targets_hbm, targets, load_sem.at[0]),
        pltpu.make_async_copy(counts_hbm, counts, load_sem.at[1]),
        pltpu.make_async_copy(pressure_hbm, pressure, load_sem.at[2]),
        pltpu.make_async_copy(basis_hbm.at[0, times], basis.at[pl.ds(0, block_len)], load_sem.at[3]),
        pltpu.make_async_copy(
            basis_hbm.at[1, times], basis.at[pl.ds(block_len, block_len)], load_sem.at[4]
        ),
        pltpu.make_async_copy(pinv_hbm, weights, load_sem.at[5]),
    ]
    for load in loads[:5]:
        load.start()
    barrier = pltpu.get_barrier_semaphore()
    for step in les_steps:
        peer = partner(les, step, les_count)
        pl.semaphore_signal(barrier, inc=1, device_id=(peer, mode), device_id_type=MESH)
    for step in mode_steps:
        peer = partner(mode, step, mode_count)
        pl.semaphore_signal(barrier, inc=1, device_id=(les, peer), device_id_type=MESH)
    loads[0].wait()
    loads[1].wait()

    target = targets[...]
    point = lax.rem(target, points_all)
    station = lax.div(target, points_all)
    owner = lax.div(point, rows_les)
    name = station * rows_les + lax.rem(point, rows_les)
    line = lax.broadcasted_iota(jnp.int32, (lines, LANES), 0)
    lane = lax.broadcasted_iota(jnp.int32, (lines, LANES), 1)
    live = line * LANES + lane < counts[0]
    owner = jnp.where(live, owner, les_count)
    first = lax.broadcasted_iota(jnp.int32, (LANES, 2 * LANES), 0)
    second = lax.broadcasted_iota(jnp.int32, (LANES, 2 * LANES), 1)
    upper = jnp.where((first <= second) | (second >= LANES), 1.0, 0.0).astype(BF16)
    above = lax.broadcasted_iota(jnp.int32, (lines, lines), 0)
    below = lax.broadcasted_iota(jnp.int32, (lines, lines), 1)
    earlier = jnp.where(above > below, 1.0, 0.0).astype(BF16)
    matches = [owner == at for at in range(les_count)]
    stacked = jnp.concatenate([jnp.where(m, 1.0, 0.0).astype(BF16) for m in matches], axis=0)
    running = jnp.dot(stacked, upper, preferred_element_type=F32)
    totals = [running[at * lines:(at + 1) * lines, LANES:] for at in range(les_count)]
    before = jnp.dot(
        earlier, jnp.concatenate(totals, axis=1).astype(BF16), preferred_element_type=F32
    )
    rank = jnp.zeros((lines, LANES), F32)
    for at in range(les_count):
        here = running[at * lines:(at + 1) * lines, :LANES] + before[:, at * LANES:(at + 1) * LANES]
        rank = jnp.where(matches[at], here, rank)
    rank = rank.astype(jnp.int32) - 1
    lines_of[...] = jnp.where(live, owner * tag_rows + lax.div(rank, LANES), -1).astype(F32)
    lanes_of[...] = lax.rem(rank, LANES).astype(F32)
    names_high[...] = lax.div(name + 1, LANES).astype(F32)
    names_low[...] = lax.rem(name + 1, LANES).astype(F32)

    source = add_places(lines, lines_of, lanes_of, slot_values, les_count * tag_rows)
    source = jnp.clip(source, 0, face_slots - 1)
    for at in range(les_count):
        sources[at] = source[at * tag_rows:(at + 1) * tag_rows]

    def id_copy(step, slot):
        return pltpu.make_async_copy(
            sources.at[partner(les, step, les_count)], source_ids.at[slot], smem_sem.at[slot]
        )

    loads[5].start()
    id_copy(les_count - 1, 0).start()
    id_copy(les_count - 2, 1).start()

    chunk = math.gcd(face_slots, 1024)
    for load in loads[2:5]:
        load.wait()
    block_basis = basis[...]

    for step in range(face_slots // chunk):
        at = pl.ds(step * chunk, chunk)
        block = pressure[at, :]
        block = jnp.concatenate([block, block], axis=1)
        spectra[at, :] = jnp.dot(block, block_basis, preferred_element_type=F32)

    pl.semaphore_wait(barrier, les_count + mode_count - 2)

    def tag_copy(step):
        peer = partner(les, step, les_count)
        return pltpu.make_async_remote_copy(
            src_ref=tags.at[peer],
            dst_ref=tags_in.at[step],
            send_sem=tag_send.at[step],
            recv_sem=tag_recv.at[step],
            device_id=(peer, mode),
            device_id_type=MESH,
        )

    def data_copy(step):
        peer = partner(les, step, les_count)
        return pltpu.make_async_remote_copy(
            src_ref=packed.at[step],
            dst_ref=data_in.at[step],
            send_sem=data_send.at[step],
            recv_sem=data_recv.at[step],
            device_id=(peer, mode),
            device_id_type=MESH,
        )

    def fill(step, slot):
        for row in range(rank_rows):
            ranks = [at * rank_rows + row for at in range(GROUPS)]
            ids = [source_ids[slot, at // LANES, at % LANES] for at in ranks]
            packed[step, pl.ds(row, 1), :] = pick([spectra[pl.ds(face, 1), :] for face in ids])

    def name_values(line_at):
        return names_high[pl.ds(line_at, 1), :], names_low[pl.ds(line_at, 1), :]

    def send_tags():
        tag = add_places(lines, lines_of, lanes_of, name_values, les_count * tag_rows)
        for at in range(les_count):
            tags[at] = tag[at * tag_rows:(at + 1) * tag_rows]
        for step in les_steps:
            tag_copy(step).start()

    @pl.loop(0, les_count // 2)
    def _(pair):
        for slot in range(2):
            step = les_count - 1 - slot - 2 * pair
            id_copy(step, slot).wait()
            fill(step, slot)

            @pl.when(pair < les_count // 2 - 1)
            def _(step=step, slot=slot):
                id_copy(step - 2, slot).start()

            if slot == 0:
                data_copy(step).start()

                @pl.when(pair == 0)
                def _():
                    send_tags()

            else:

                @pl.when(step > 0)
                def _(step=step):
                    data_copy(step).start()

    for step in range(les_count):
        if step > 0:
            tag_copy(step).wait()
        found = (tags[les] if step == 0 else tags_in[step]) - 1
        at = pl.ds(step * tag_rows, tag_rows)
        tag_lines[at, :] = (found >> 7).astype(F32)
        tag_lanes[at, :] = (found & (LANES - 1)).astype(F32)
    found = add_places(les_count * tag_rows, tag_lines, tag_lanes, slot_values, dense)
    inverse[...] = jnp.clip(found, 0, les_count * cap - 1)
    for of in range(stations):
        for step in range(mode_count):
            start = (of * mode_count + partner(mode, step, mode_count)) * mode_lines
            ordered[pl.ds((of * mode_count + step) * mode_lines, mode_lines), :] = (
                inverse[pl.ds(start, mode_lines), :]
            )
    inverse_copy = pltpu.make_async_copy(ordered, point_ids, smem_sem.at[2])
    inverse_copy.start()

    from_lane = lax.broadcasted_iota(jnp.int32, (LANES, GROUPS * LANES), 0)
    to_lane = lax.broadcasted_iota(jnp.int32, (LANES, GROUPS * LANES), 1)
    wanted = (to_lane // LANES) * COLS + to_lane % COLS
    repeat = jnp.where(from_lane == wanted, 1.0, 0.0).astype(BF16)
    repeat = jnp.concatenate([repeat, repeat], axis=0)
    steps = (0, *les_steps)
    for first_step in range(0, les_count, WIDEN):
        batch = steps[first_step:first_step + WIDEN]
        held = []
        for step in batch:
            if step > 0:
                data_copy(step).wait()
            high, low = split(data_in[step] if step > 0 else packed[0])
            held.append(jnp.concatenate([high, low], axis=1))
        wide = jnp.dot(jnp.concatenate(held, axis=0), repeat, preferred_element_type=F32)
        for index, step in enumerate(batch):
            for at in range(GROUPS):
                spread[pl.ds(step * cap + at * rank_rows, rank_rows), :] = wide[
                    index * rank_rows:(index + 1) * rank_rows, at * LANES:(at + 1) * LANES
                ]
    inverse_copy.wait()

    def block_copy(of, step):
        return pltpu.make_async_remote_copy(
            src_ref=blocks.at[of, step],
            dst_ref=blocks_in.at[of, step],
            send_sem=block_send.at[of, step],
            recv_sem=block_recv.at[of, step],
            device_id=(les, partner(mode, step, mode_count)),
            device_id_type=MESH,
        )

    def gather(of, step):
        start = (of * mode_count + step) * mode_lines
        for row in range(block_rows):
            points = [at * block_rows + row for at in range(GROUPS)]
            ids = [point_ids[start + at // LANES, at % LANES] for at in points]
            blocks[of, step, pl.ds(row, 1), :] = pick([spread[pl.ds(place, 1), :] for place in ids])

    for of in range(stations):
        for step in mode_steps:
            gather(of, step)
            block_copy(of, step).start()
    for of in range(stations):
        gather(of, 0)

    loads[5].wait()
    tiles = mode_total // LANES
    width = out.shape[2]
    les_width = mode_count * width
    span = sums_in.shape[2]

    def sum_copy(of, step):
        peer = partner(les, step, les_count)
        start = share_start(peer, les_width, tiles, span)
        return pltpu.make_async_remote_copy(
            src_ref=product.at[of, pl.ds(start, span)],
            dst_ref=sums_in.at[of, step],
            send_sem=sum_send.at[of, step],
            recv_sem=sum_recv.at[of, step],
            device_id=(peer, mode),
            device_id_type=MESH,
        )

    for of in range(stations):
        total = blocks[of, 0]
        for step in mode_steps:
            block_copy(of, step).wait()
            total = total + blocks_in[of, step]
        high = total.astype(BF16).astype(F32)
        turned = []
        for half in (high, total - high):
            both = jnp.concatenate([half, pltpu.roll(half, LANES - COLS, 1)], axis=0).T
            pairs = [both[at * COLS:(at + 1) * COLS, :] for at in range(0, GROUPS, 2)]
            turned.append(jnp.concatenate(pairs, axis=1))
        turned = jnp.concatenate(turned, axis=0).astype(BF16)
        result = lax.dot_general(
            turned, weights[of], (((1,), (1,)), ((), ())), preferred_element_type=F32
        )
        result = result[:COLS] + result[COLS:]
        for tile in range(tiles):
            product[of, tile] = result[:, tile * LANES:(tile + 1) * LANES]
        for step in les_steps:
            sum_copy(of, step).start()

    own_start = share_start(les, les_width, tiles, span)
    own = []
    for of in range(stations):
        total = product[of, pl.ds(own_start, span)]
        for step in les_steps:
            sum_copy(of, step).wait()
            total = total + sums_in[of, step]
        own.append(jnp.concatenate([total[at] for at in range(span)], axis=1))

    offset = les * les_width - own_start * LANES
    lane = lax.broadcasted_iota(jnp.int32, (COLS, LANES), 1)

    def last_copy(step):
        return pltpu.make_async_remote_copy(
            src_ref=shares.at[step],
            dst_ref=last_in.at[step],
            send_sem=last_send.at[step],
            recv_sem=last_recv.at[step],
            device_id=(les, partner(mode, step, mode_count)),
            device_id_type=MESH,
        )

    for step in (*mode_steps, 0):
        at = offset + partner(mode, step, mode_count) * width
        turn = lax.rem(span * LANES - at, span * LANES)
        one = pltpu.roll(own[0], turn, 1)[:, :LANES]
        two = pltpu.roll(own[1], lax.rem(turn + width, span * LANES), 1)[:, :LANES]
        shares[step] = jnp.where(lane < width, one, two)
        if step > 0:
            last_copy(step).start()
    total = shares[0]
    for step in mode_steps:
        last_copy(step).wait()
        total = total + last_in[step]
    out[0] = total[:, :width]
    out[1] = pltpu.roll(total, LANES - width, 1)[:, :width]


def local(pressure, targets, counts, pseudo_inverse):
    les_count = lax.axis_size("les")
    mode_count = lax.axis_size("modes")
    face_slots, block_len = pressure.shape
    stations, mode_total, point_dev = pseudo_inverse.shape
    lines = face_slots // LANES
    cap = face_slots // les_count
    rank_rows = cap // GROUPS
    tag_rows = cap // LANES
    dense = stations * point_dev * mode_count // LANES
    block_rows = point_dev // GROUPS
    width = mode_total // (les_count * mode_count)
    les_width = width * mode_count
    tiles = mode_total // LANES
    span = max(
        ((at + 1) * les_width - 1) // LANES - at * les_width // LANES + 1 for at in range(les_count)
    )
    anywhere = pl.BlockSpec(memory_space=pl.ANY)
    dma = pltpu.SemaphoreType.DMA
    vmem = pltpu.VMEM
    result = pl.pallas_call(
        functools.partial(kernel, les_count, mode_count),
        out_shape=jax.ShapeDtypeStruct((stations, COLS, width), F32),
        in_specs=[anywhere] * 5,
        out_specs=pl.BlockSpec(memory_space=pltpu.VMEM),
        scratch_shapes=[
            pltpu.SMEM((1,), jnp.int32),
            vmem((lines, LANES), jnp.int32),
            vmem((face_slots, block_len), BF16),
            vmem((2 * block_len, LANES), BF16),
            vmem((stations, mode_total, point_dev), BF16),
            vmem((lines, LANES), F32),
            vmem((lines, LANES), F32),
            vmem((lines, LANES), F32),
            vmem((lines, LANES), F32),
            vmem((les_count, tag_rows, LANES), jnp.int32),
            vmem((les_count, tag_rows, LANES), jnp.int32),
            vmem((les_count, tag_rows, LANES), jnp.int32),
            vmem((les_count * tag_rows, LANES), F32),
            vmem((les_count * tag_rows, LANES), F32),
            vmem((dense, LANES), jnp.int32),
            vmem((dense, LANES), jnp.int32),
            pltpu.SMEM((2, tag_rows, LANES), jnp.int32),
            pltpu.SMEM((dense, LANES), jnp.int32),
            vmem((face_slots, LANES), F32),
            vmem((les_count, rank_rows, LANES), F32),
            vmem((les_count, rank_rows, LANES), F32),
            vmem((les_count * cap, LANES), F32),
            vmem((stations, mode_count, block_rows, LANES), F32),
            vmem((stations, mode_count, block_rows, LANES), F32),
            vmem((stations, tiles, COLS, LANES), F32),
            vmem((stations, les_count, span, COLS, LANES), F32),
            vmem((mode_count, COLS, LANES), F32),
            vmem((mode_count, COLS, LANES), F32),
            dma((6,)),
            dma((3,)),
            dma((les_count,)),
            dma((les_count,)),
            dma((les_count,)),
            dma((les_count,)),
            dma((stations, mode_count)),
            dma((stations, mode_count)),
            dma((stations, les_count)),
            dma((stations, les_count)),
            dma((mode_count,)),
            dma((mode_count,)),
        ],
        compiler_params=pltpu.CompilerParams(
            collective_id=0, has_side_effects=True, vmem_limit_bytes=VMEM_BYTES
        ),
        name="harmonics",
    )(
        counts, targets.reshape(lines, LANES), pressure,
        jnp.asarray(fourier_columns()), pseudo_inverse,
    )
    return result.reshape(stations, 2, HARM, width)


def solution(mesh):
    placed = (P("les", "modes"), P("les"), P("les"), P(None, None, ("les", "modes")))
    return jax.shard_map(
        local,
        mesh=mesh,
        in_specs=placed,
        out_specs=P(None, None, None, ("les", "modes")),
        check_vma=False,
    )
```

```python
import functools
import math

import jax
import jax.numpy as jnp
import numpy as np
from jax import lax
from jax.experimental import pallas as pl
from jax.experimental.pallas import tpu as pltpu
from jax.sharding import PartitionSpec as P

TIME = 512
HARM = 8
COLS = 2 * HARM
LANES = 128
GROUPS = LANES // COLS
GROUP_LINES = 64
WIDEN = 4
VMEM_BYTES = 56 * 1024 * 1024
MESH = pl.DeviceIdType.MESH
F32 = jnp.float32
BF16 = jnp.bfloat16


def fourier_columns():
    phase_ids = np.arange(TIME)[:, None] * np.arange(1, HARM + 1)[None, :] % TIME
    angles = phase_ids * (2.0 * math.pi / TIME)
    columns = np.concatenate([np.cos(angles), -np.sin(angles)], axis=1) * math.sqrt(2.0 / TIME)
    columns = np.tile(columns, (1, GROUPS)).astype(np.float32)
    high = columns.astype(jnp.bfloat16)
    low = (columns - high.astype(np.float32)).astype(jnp.bfloat16)
    return np.stack([high, low])


def partner(index, step, count):
    total, bit = 0, 1
    while bit < count:
        total = total + lax.rem(lax.rem(lax.div(index, bit), 2) + (step // bit) % 2, 2) * bit
        bit *= 2
    return total


def pick(rows):
    group = lax.broadcasted_iota(jnp.int32, (1, LANES), 1) // COLS
    bit = 1
    while len(rows) > 1:
        even = (group // bit) % 2 == 0
        rows = [jnp.where(even, rows[at], rows[at + 1]) for at in range(0, len(rows), 2)]
        bit *= 2
    return rows[0]


def split(value):
    high = value.astype(BF16)
    return high, (value - high.astype(F32)).astype(BF16)


def add_places(line_count, lines_of, lanes_of, values_of, out_lines):
    out_ids = lax.broadcasted_iota(jnp.int32, (out_lines, LANES), 0).astype(F32).astype(BF16)
    lane_ids = lax.broadcasted_iota(jnp.int32, (LANES, LANES), 0).astype(F32).astype(BF16)
    one, zero = jnp.ones((), BF16), jnp.zeros((), BF16)

    def add(step, total):
        lefts, rights = [], []
        for at in range(GROUP_LINES):
            line_at = step * GROUP_LINES + at

            def spread_row(row, rows):
                return jnp.broadcast_to(row.astype(BF16), (rows, LANES))

            hit = lane_ids == spread_row(lanes_of[pl.ds(line_at, 1), :], LANES)
            left = out_ids == spread_row(lines_of[pl.ds(line_at, 1), :], out_lines)
            values = [spread_row(row, out_lines) for row in values_of(line_at)]
            lefts.append(jnp.concatenate([jnp.where(left, value, zero) for value in values], axis=0))
            rights.append(jnp.where(hit, one, zero))
        return total + lax.dot_general(
            jnp.concatenate(rights, axis=1), jnp.concatenate(lefts, axis=1),
            (((1,), (1,)), ((), ())), preferred_element_type=F32,
        )

    total = lax.fori_loop(
        0, line_count // GROUP_LINES, add, jnp.zeros((LANES, 2 * out_lines), F32)
    ).T
    return (total[:out_lines] * LANES + total[out_lines:]).astype(jnp.int32)


def slot_values(line_at):
    line = jnp.full((1, LANES), line_at, jnp.int32).astype(F32)
    return line, lax.broadcasted_iota(jnp.int32, (1, LANES), 1).astype(F32)


def mixed(step):
    return jnp.where(step == 3, 4, jnp.where(step == 4, 3, step))


def share_start(les, les_width, tiles, span):
    return jnp.minimum(lax.div(les * les_width, LANES), tiles - span)


def kernel(
    les_count, mode_count, counts_hbm, targets_hbm, pressure_hbm, basis_hbm, pinv_hbm, out,
    counts, targets, pressure, basis, weights, lines_of, lanes_of, names_high, names_low,
    sources, tags, tags_in, tag_lines, tag_lanes, inverse, ordered, source_ids, point_ids,
    spectra, packed, data_in, spread, blocks, blocks_in,
    product, sums_in, shares, last_in,
    load_sem, smem_sem, tag_send, tag_recv, data_send, data_recv,
    block_send, block_recv, sum_send, sum_recv, last_send, last_recv,
):
    les, mode = lax.axis_index("les"), lax.axis_index("modes")
    face_slots, block_len = pressure.shape
    stations, mode_total, point_dev = weights.shape
    rows_les = point_dev * mode_count
    points_all = rows_les * les_count
    lines = face_slots // LANES
    cap = face_slots // les_count
    tag_rows = cap // LANES
    rank_rows = cap // GROUPS
    dense = stations * rows_les // LANES
    mode_lines = point_dev // LANES
    block_rows = point_dev // GROUPS
    les_steps = range(les_count - 1, 0, -1)
    mode_steps = range(mode_count - 1, 0, -1)

    times = pl.ds(pl.multiple_of(mode * block_len, block_len), block_len)
    loads = [
        pltpu.make_async_copy(targets_hbm, targets, load_sem.at[0]),
        pltpu.make_async_copy(counts_hbm, counts, load_sem.at[1]),
        pltpu.make_async_copy(pressure_hbm, pressure, load_sem.at[2]),
        pltpu.make_async_copy(basis_hbm.at[0, times], basis.at[pl.ds(0, block_len)], load_sem.at[3]),
        pltpu.make_async_copy(
            basis_hbm.at[1, times], basis.at[pl.ds(block_len, block_len)], load_sem.at[4]
        ),
        pltpu.make_async_copy(pinv_hbm, weights, load_sem.at[5]),
    ]
    for load in loads[:5]:
        load.start()
    barrier = pltpu.get_barrier_semaphore()
    for step in les_steps:
        peer = partner(les, step, les_count)
        pl.semaphore_signal(barrier, inc=1, device_id=(peer, mode), device_id_type=MESH)
    for step in mode_steps:
        peer = partner(mode, step, mode_count)
        pl.semaphore_signal(barrier, inc=1, device_id=(les, peer), device_id_type=MESH)
    loads[0].wait()
    loads[1].wait()

    target = targets[...]
    point = lax.rem(target, points_all)
    station = lax.div(target, points_all)
    owner = lax.div(point, rows_les)
    name = station * rows_les + lax.rem(point, rows_les)
    line = lax.broadcasted_iota(jnp.int32, (lines, LANES), 0)
    lane = lax.broadcasted_iota(jnp.int32, (lines, LANES), 1)
    live = line * LANES + lane < counts[0]
    owner = jnp.where(live, owner, les_count)
    first = lax.broadcasted_iota(jnp.int32, (LANES, 2 * LANES), 0)
    second = lax.broadcasted_iota(jnp.int32, (LANES, 2 * LANES), 1)
    upper = jnp.where((first <= second) | (second >= LANES), 1.0, 0.0).astype(BF16)
    above = lax.broadcasted_iota(jnp.int32, (lines, lines), 0)
    below = lax.broadcasted_iota(jnp.int32, (lines, lines), 1)
    earlier = jnp.where(above > below, 1.0, 0.0).astype(BF16)
    matches = [owner == at for at in range(les_count)]
    stacked = jnp.concatenate([jnp.where(m, 1.0, 0.0).astype(BF16) for m in matches], axis=0)
    running = jnp.dot(stacked, upper, preferred_element_type=F32)
    totals = [running[at * lines:(at + 1) * lines, LANES:] for at in range(les_count)]
    before = jnp.dot(
        earlier, jnp.concatenate(totals, axis=1).astype(BF16), preferred_element_type=F32
    )
    rank = jnp.zeros((lines, LANES), F32)
    for at in range(les_count):
        here = running[at * lines:(at + 1) * lines, :LANES] + before[:, at * LANES:(at + 1) * LANES]
        rank = jnp.where(matches[at], here, rank)
    rank = rank.astype(jnp.int32) - 1
    lines_of[...] = jnp.where(live, owner * tag_rows + lax.div(rank, LANES), -1).astype(F32)
    lanes_of[...] = lax.rem(rank, LANES).astype(F32)
    names_high[...] = lax.div(name + 1, LANES).astype(F32)
    names_low[...] = lax.rem(name + 1, LANES).astype(F32)

    source = add_places(lines, lines_of, lanes_of, slot_values, les_count * tag_rows)
    source = jnp.clip(source, 0, face_slots - 1)
    for at in range(les_count):
        sources[at] = source[at * tag_rows:(at + 1) * tag_rows]

    def id_copy(step, slot):
        return pltpu.make_async_copy(
            sources.at[partner(les, step, les_count)], source_ids.at[slot], smem_sem.at[slot]
        )

    loads[5].start()
    id_copy(les_count - 1, 0).start()
    id_copy(les_count - 2, 1).start()

    chunk = math.gcd(face_slots, 1024)
    for load in loads[2:5]:
        load.wait()
    block_basis = basis[...]

    for step in range(face_slots // chunk):
        at = pl.ds(step * chunk, chunk)
        block = pressure[at, :]
        block = jnp.concatenate([block, block], axis=1)
        spectra[at, :] = jnp.dot(block, block_basis, preferred_element_type=F32)

    pl.semaphore_wait(barrier, les_count + mode_count - 2)

    def tag_copy(step):
        peer = partner(les, step, les_count)
        return pltpu.make_async_remote_copy(
            src_ref=tags.at[peer],
            dst_ref=tags_in.at[step],
            send_sem=tag_send.at[step],
            recv_sem=tag_recv.at[step],
            device_id=(peer, mode),
            device_id_type=MESH,
        )

    def data_copy(step):
        peer = partner(les, step, les_count)
        return pltpu.make_async_remote_copy(
            src_ref=packed.at[step],
            dst_ref=data_in.at[step],
            send_sem=data_send.at[step],
            recv_sem=data_recv.at[step],
            device_id=(peer, mode),
            device_id_type=MESH,
        )

    def fill(step, slot):
        for row in range(rank_rows):
            ranks = [at * rank_rows + row for at in range(GROUPS)]
            ids = [source_ids[slot, at // LANES, at % LANES] for at in ranks]
            packed[step, pl.ds(row, 1), :] = pick([spectra[pl.ds(face, 1), :] for face in ids])

    def name_values(line_at):
        return names_high[pl.ds(line_at, 1), :], names_low[pl.ds(line_at, 1), :]

    def send_tags():
        tag = add_places(lines, lines_of, lanes_of, name_values, les_count * tag_rows)
        for at in range(les_count):
            tags[at] = tag[at * tag_rows:(at + 1) * tag_rows]
        for step in les_steps:
            tag_copy(step).start()

    @pl.loop(0, les_count // 2)
    def _(pair):
        for slot in range(2):
            raw = les_count - 1 - slot - 2 * pair
            step = mixed(raw)
            id_copy(step, slot).wait()
            fill(step, slot)

            @pl.when(pair < les_count // 2 - 1)
            def _(raw=raw, slot=slot):
                id_copy(mixed(raw - 2), slot).start()

            if slot == 0:
                data_copy(step).start()

                @pl.when(pair == 0)
                def _():
                    send_tags()

            else:

                @pl.when(step > 0)
                def _(step=step):
                    data_copy(step).start()

    for step in range(les_count):
        if step > 0:
            tag_copy(step).wait()
        found = (tags[les] if step == 0 else tags_in[step]) - 1
        at = pl.ds(step * tag_rows, tag_rows)
        tag_lines[at, :] = (found >> 7).astype(F32)
        tag_lanes[at, :] = (found & (LANES - 1)).astype(F32)
    found = add_places(les_count * tag_rows, tag_lines, tag_lanes, slot_values, dense)
    inverse[...] = jnp.clip(found, 0, les_count * cap - 1)
    for of in range(stations):
        for step in range(mode_count):
            start = (of * mode_count + partner(mode, step, mode_count)) * mode_lines
            ordered[pl.ds((of * mode_count + step) * mode_lines, mode_lines), :] = (
                inverse[pl.ds(start, mode_lines), :]
            )
    inverse_copy = pltpu.make_async_copy(ordered, point_ids, smem_sem.at[2])
    inverse_copy.start()

    from_lane = lax.broadcasted_iota(jnp.int32, (LANES, GROUPS * LANES), 0)
    to_lane = lax.broadcasted_iota(jnp.int32, (LANES, GROUPS * LANES), 1)
    wanted = (to_lane // LANES) * COLS + to_lane % COLS
    repeat = jnp.where(from_lane == wanted, 1.0, 0.0).astype(BF16)
    repeat = jnp.concatenate([repeat, repeat], axis=0)
    steps = (0, *les_steps)
    for first_step in range(0, les_count, WIDEN):
        batch = steps[first_step:first_step + WIDEN]
        held = []
        for step in batch:
            if step > 0:
                data_copy(step).wait()
            high, low = split(data_in[step] if step > 0 else packed[0])
            held.append(jnp.concatenate([high, low], axis=1))
        wide = jnp.dot(jnp.concatenate(held, axis=0), repeat, preferred_element_type=F32)
        for index, step in enumerate(batch):
            for at in range(GROUPS):
                spread[pl.ds(step * cap + at * rank_rows, rank_rows), :] = wide[
                    index * rank_rows:(index + 1) * rank_rows, at * LANES:(at + 1) * LANES
                ]
    inverse_copy.wait()

    def block_copy(of, step):
        return pltpu.make_async_remote_copy(
            src_ref=blocks.at[of, step],
            dst_ref=blocks_in.at[of, step],
            send_sem=block_send.at[of, step],
            recv_sem=block_recv.at[of, step],
            device_id=(les, partner(mode, step, mode_count)),
            device_id_type=MESH,
        )

    def gather(of, step):
        start = (of * mode_count + step) * mode_lines
        for row in range(block_rows):
            points = [at * block_rows + row for at in range(GROUPS)]
            ids = [point_ids[start + at // LANES, at % LANES] for at in points]
            blocks[of, step, pl.ds(row, 1), :] = pick([spread[pl.ds(place, 1), :] for place in ids])

    for of in range(stations):
        for step in mode_steps:
            gather(of, step)
            block_copy(of, step).start()
    for of in range(stations):
        gather(of, 0)

    loads[5].wait()
    tiles = mode_total // LANES
    width = out.shape[2]
    les_width = mode_count * width
    span = sums_in.shape[2]

    def sum_copy(of, step):
        peer = partner(les, step, les_count)
        start = share_start(peer, les_width, tiles, span)
        return pltpu.make_async_remote_copy(
            src_ref=product.at[of, pl.ds(start, span)],
            dst_ref=sums_in.at[of, step],
            send_sem=sum_send.at[of, step],
            recv_sem=sum_recv.at[of, step],
            device_id=(peer, mode),
            device_id_type=MESH,
        )

    for of in range(stations):
        total = blocks[of, 0]
        for step in mode_steps:
            block_copy(of, step).wait()
            total = total + blocks_in[of, step]
        high = total.astype(BF16).astype(F32)
        turned = []
        for half in (high, total - high):
            both = jnp.concatenate([half, pltpu.roll(half, LANES - COLS, 1)], axis=0).T
            pairs = [both[at * COLS:(at + 1) * COLS, :] for at in range(0, GROUPS, 2)]
            turned.append(jnp.concatenate(pairs, axis=1))
        turned = jnp.concatenate(turned, axis=0).astype(BF16)
        result = lax.dot_general(
            turned, weights[of], (((1,), (1,)), ((), ())), preferred_element_type=F32
        )
        result = result[:COLS] + result[COLS:]
        for tile in range(tiles):
            product[of, tile] = result[:, tile * LANES:(tile + 1) * LANES]
        for step in les_steps:
            sum_copy(of, step).start()

    own_start = share_start(les, les_width, tiles, span)
    own = []
    for of in range(stations):
        total = product[of, pl.ds(own_start, span)]
        for step in les_steps:
            sum_copy(of, step).wait()
            total = total + sums_in[of, step]
        own.append(jnp.concatenate([total[at] for at in range(span)], axis=1))

    offset = les * les_width - own_start * LANES
    lane = lax.broadcasted_iota(jnp.int32, (COLS, LANES), 1)

    def last_copy(step):
        return pltpu.make_async_remote_copy(
            src_ref=shares.at[step],
            dst_ref=last_in.at[step],
            send_sem=last_send.at[step],
            recv_sem=last_recv.at[step],
            device_id=(les, partner(mode, step, mode_count)),
            device_id_type=MESH,
        )

    for step in (*mode_steps, 0):
        at = offset + partner(mode, step, mode_count) * width
        turn = lax.rem(span * LANES - at, span * LANES)
        one = pltpu.roll(own[0], turn, 1)[:, :LANES]
        two = pltpu.roll(own[1], lax.rem(turn + width, span * LANES), 1)[:, :LANES]
        shares[step] = jnp.where(lane < width, one, two)
        if step > 0:
            last_copy(step).start()
    total = shares[0]
    for step in mode_steps:
        last_copy(step).wait()
        total = total + last_in[step]
    out[0] = total[:, :width]
    out[1] = pltpu.roll(total, LANES - width, 1)[:, :width]


def local(pressure, targets, counts, pseudo_inverse):
    les_count = lax.axis_size("les")
    mode_count = lax.axis_size("modes")
    face_slots, block_len = pressure.shape
    stations, mode_total, point_dev = pseudo_inverse.shape
    lines = face_slots // LANES
    cap = face_slots // les_count
    rank_rows = cap // GROUPS
    tag_rows = cap // LANES
    dense = stations * point_dev * mode_count // LANES
    block_rows = point_dev // GROUPS
    width = mode_total // (les_count * mode_count)
    les_width = width * mode_count
    tiles = mode_total // LANES
    span = max(
        ((at + 1) * les_width - 1) // LANES - at * les_width // LANES + 1 for at in range(les_count)
    )
    anywhere = pl.BlockSpec(memory_space=pl.ANY)
    dma = pltpu.SemaphoreType.DMA
    vmem = pltpu.VMEM
    result = pl.pallas_call(
        functools.partial(kernel, les_count, mode_count),
        out_shape=jax.ShapeDtypeStruct((stations, COLS, width), F32),
        in_specs=[anywhere] * 5,
        out_specs=pl.BlockSpec(memory_space=pltpu.VMEM),
        scratch_shapes=[
            pltpu.SMEM((1,), jnp.int32),
            vmem((lines, LANES), jnp.int32),
            vmem((face_slots, block_len), BF16),
            vmem((2 * block_len, LANES), BF16),
            vmem((stations, mode_total, point_dev), BF16),
            vmem((lines, LANES), F32),
            vmem((lines, LANES), F32),
            vmem((lines, LANES), F32),
            vmem((lines, LANES), F32),
            vmem((les_count, tag_rows, LANES), jnp.int32),
            vmem((les_count, tag_rows, LANES), jnp.int32),
            vmem((les_count, tag_rows, LANES), jnp.int32),
            vmem((les_count * tag_rows, LANES), F32),
            vmem((les_count * tag_rows, LANES), F32),
            vmem((dense, LANES), jnp.int32),
            vmem((dense, LANES), jnp.int32),
            pltpu.SMEM((2, tag_rows, LANES), jnp.int32),
            pltpu.SMEM((dense, LANES), jnp.int32),
            vmem((face_slots, LANES), F32),
            vmem((les_count, rank_rows, LANES), F32),
            vmem((les_count, rank_rows, LANES), F32),
            vmem((les_count * cap, LANES), F32),
            vmem((stations, mode_count, block_rows, LANES), F32),
            vmem((stations, mode_count, block_rows, LANES), F32),
            vmem((stations, tiles, COLS, LANES), F32),
            vmem((stations, les_count, span, COLS, LANES), F32),
            vmem((mode_count, COLS, LANES), F32),
            vmem((mode_count, COLS, LANES), F32),
            dma((6,)),
            dma((3,)),
            dma((les_count,)),
            dma((les_count,)),
            dma((les_count,)),
            dma((les_count,)),
            dma((stations, mode_count)),
            dma((stations, mode_count)),
            dma((stations, les_count)),
            dma((stations, les_count)),
            dma((mode_count,)),
            dma((mode_count,)),
        ],
        compiler_params=pltpu.CompilerParams(
            collective_id=0, has_side_effects=True, vmem_limit_bytes=VMEM_BYTES
        ),
        name="harmonics",
    )(
        counts, targets.reshape(lines, LANES), pressure,
        jnp.asarray(fourier_columns()), pseudo_inverse,
    )
    return result.reshape(stations, 2, HARM, width)


def solution(mesh):
    placed = (P("les", "modes"), P("les"), P("les"), P(None, None, ("les", "modes")))
    return jax.shard_map(
        local,
        mesh=mesh,
        in_specs=placed,
        out_specs=P(None, None, None, ("les", "modes")),
        check_vma=False,
    )
```
